32 devices in a mesh: dp: 16 (over z, y, x), head: 2 (over core).
Axes of the slice: x: 2, y: 2, z: 4, core: 2. Of those that a mesh axis runs over, the one named last changes fastest.
Arguments:
- hidden_states: bfloat16 [32768, 768], P(('dp', 'head')), may hold values from -6 to 6
- segment_ids: int32 [32768], P(('dp', 'head')), may hold values from -1 to 1023, as said below
- input_weight: bfloat16 [768, 2304], P('dp'), may hold values from -0.21875 to 0.21875
- output_weight: bfloat16 [768, 768], P('dp'), may hold values from -0.5 to 0.5
- expand_weight: bfloat16 [768, 3072], P('dp'), may hold values from -0.21875 to 0.21875
- reduce_weight: bfloat16 [3072, 768], P('dp'), may hold values from -0.15625 to 0.15625
- adapter_down: bfloat16 [2, 768, 64], replicated, may hold values from -0.21875 to 0.21875
- adapter_down_bias: float32 [2, 64], replicated, may hold values from -3 to 3
- adapter_up: bfloat16 [2, 64, 768], replicated, may hold values from -1 to 1
- adapter_up_bias: float32 [2, 768], replicated, may hold values from -2 to 2
- norm_gain: float32 [2, 768], replicated, may hold values from 0.5 to 1.5
- norm_shift: float32 [2, 768], replicated, may hold values from -2 to 2
- output_grad: bfloat16 [32768, 768], P(('dp', 'head')), may hold values from -6 to 6
Outputs:
- layer_output: bfloat16 [32768, 768], P(('dp', 'head'))
- input_grad: float32 [32768, 768], P(('dp', 'head'))
- norm_ratio: float32 [2], replicated
- down_grad: float32 [2, 768, 64], replicated
- down_bias_grad: float32 [2, 64], replicated
- up_grad: float32 [2, 64, 768], replicated
- up_bias_grad: float32 [2, 768], replicated
- gain_grad: float32 [2, 768], replicated
- shift_grad: float32 [2, 768], replicated
The draws below stay inside these ranges and needn't reach their ends.
Inputs may be any that keep to these rules, and one draw needn't show every extreme that they name: `segment_ids`: in each sequence of 512 positions the valid positions come first (a multiple of 32) and the rest carry -1; a valid position of sequence s carries s * 16 (512 / 32) plus the number of its item within the sequence; items hold 32 positions, or one item covers the whole sequence.
All inputs are finite; a program needn't handle non-finite values.
Results may differ from the reference program's by a relative error of at most 0.015.
Values may be sent and summed in bfloat16 or wider, within the bound.
A program may use at most 192 MiB of HBM per device.

```python
import jax
import jax.numpy as jnp
from jax import lax

D = 768
FF = 3072
HEADS = 12
HEAD_DIM = 64
R = 64
SEQ_LEN = 512
ITEM = 32
SEQS = 64
TOKENS = 32768


def draw_segment_ids(key, part):
    item_count = SEQ_LEN // ITEM
    key_length, key_whole = jax.random.split(key)
    seq_index = jnp.arange(SEQS)
    lengths = ITEM * jax.random.randint(key_length, (SEQS,), 2, item_count + 1)
    whole_seq = jax.random.randint(key_whole, (SEQS,), 0, 8) == 0
    whole_seq = whole_seq & (seq_index > 0) & (seq_index < SEQS - 1)
    lengths = jnp.where(whole_seq | (seq_index == SEQS - 1), SEQ_LEN, lengths)
    lengths = jnp.where(seq_index == 0, SEQ_LEN // 2, lengths)
    positions = jnp.arange(SEQ_LEN)
    item_of = jnp.where(whole_seq[:, None], 0, positions[None, :] // ITEM)
    numbers = seq_index[:, None] * item_count + item_of
    numbers = jnp.where(positions[None, :] < lengths[:, None], numbers, -1)
    return numbers.reshape(SEQS * SEQ_LEN).astype(jnp.int32)


def shard_levels(rng, dims, pieces, low, largest):
    gain = 1.0
    for dim, shards_of in pieces:
        draws = jax.random.uniform(jax.random.fold_in(jax.random.fold_in(rng, 6), dim), (shards_of,), jnp.float32, low / len(pieces), largest / len(pieces))
        gain = gain * jnp.repeat(jnp.exp(draws), dims[dim] // shards_of).reshape((-1,) + (1,) * (len(dims) - 1 - dim))
    return gain


def bell_draw(own_key, shape, deviation, reach, shards=(), kind=jnp.bfloat16):
    entries = jax.random.normal(own_key, shape, jnp.float32) * deviation
    if len(shards) > 0:
        entries = shard_levels(own_key, shape, shards, -0.22, 0.18) * entries
    return jnp.clip(entries, min=-reach, max=reach).astype(kind)


def setup_inputs(seed: int = 0) -> dict:
    seeds = jax.random.split(jax.random.key(seed), 14)
    return {
        "hidden_states": bell_draw(seeds[0], (TOKENS, D), 1.0, 6.0, ((0, 32),)),
        "segment_ids": draw_segment_ids(jax.random.fold_in(seeds[13], 71), 0),
        "input_weight": bell_draw(seeds[2], (D, 3 * D), D ** -0.5, 0.21875, ((0, 16),)),
        "output_weight": bell_draw(seeds[3], (D, D), 128 ** -0.5, 0.5, ((0, 16),)),
        "expand_weight": bell_draw(seeds[4], (D, FF), D ** -0.5, 0.21875, ((0, 16),)),
        "reduce_weight": bell_draw(seeds[5], (FF, D), (FF // 2) ** -0.5, 0.15625, ((0, 16),)),
        "adapter_down": bell_draw(seeds[6], (2, D, R), D ** -0.5, 0.21875),
        "adapter_down_bias": bell_draw(seeds[7], (2, R), 0.5, 3.0, (), jnp.float32),
        "adapter_up": bell_draw(seeds[8], (2, R, D), (R // 2) ** -0.5, 1.0),
        "adapter_up_bias": bell_draw(seeds[9], (2, D), 0.3, 2.0, (), jnp.float32),
        "norm_gain": jnp.clip(1.0 + 0.1 * jax.random.normal(seeds[10], (2, D), jnp.float32), 0.5, 1.5),
        "norm_shift": bell_draw(seeds[11], (2, D), 0.3, 2.0, (), jnp.float32),
        "output_grad": bell_draw(seeds[12], (TOKENS, D), 1.0, 6.0, ((0, 32),)),
    }


EPS_NORM = 1e-12
EPS_RATIO = 1e-06
SCORE_SCALE = 0.125
PRECISE = lax.Precision.HIGHEST

@jax.custom_vjp
def low(v):
    return lax.optimization_barrier(v.astype(jnp.bfloat16)).astype(jnp.float32)

@jax.custom_vjp
def low_back(v):
    return v

def low_keep(v):
    return (low(v), None)

def low_pass(kept, grad):
    return (grad,)

def back_keep(v):
    return (v, None)

def back_low(kept, grad):
    return (low(grad),)
low.defvjp(low_keep, low_pass)
low_back.defvjp(back_keep, back_low)

def matmul_high(left_side, right_side):
    return jnp.dot(left_side, right_side, precision=PRECISE, preferred_element_type=jnp.float32)

def layer_norm(values, gain_row, shift_row):
    centred = values - lax.optimization_barrier(jnp.mean(values, axis=-1, keepdims=True))
    variance = lax.optimization_barrier(jnp.mean(centred * centred, axis=-1, keepdims=True))
    return centred * lax.rsqrt(variance + EPS_NORM) * gain_row + shift_row

def gelu_exact(values):
    return jax.nn.gelu(values, approximate=False)

def attend_one(seq_block):
    queries, key_rows, value_rows, segment = seq_block
    scores = low_back(jnp.einsum('qhd,khd->hqk', queries, key_rows, precision=PRECISE) * SCORE_SCALE)
    positions = jnp.arange(SEQ_LEN)
    allowed = (segment[:, None] == segment[None, :]) & (segment[None, :] >= 0) | (positions[:, None] == positions[None, :])
    scores = jnp.where(allowed[None], scores, -1e+30)
    row_max = lax.optimization_barrier(jnp.max(scores, axis=-1, keepdims=True))
    exponents = jnp.exp(scores - row_max)
    attn_probs = low(exponents / lax.optimization_barrier(jnp.sum(exponents, axis=-1, keepdims=True)))
    return jnp.einsum('hqk,khd->qhd', attn_probs, value_rows, precision=PRECISE)

def adapter(inputs, down_proj, down_bias, up_proj, up_bias):
    hidden = low_back(matmul_high(low(inputs), down_proj) + down_bias)
    branch = low_back(matmul_high(low(gelu_exact(hidden)), up_proj) + up_bias)
    ratio_row = jnp.sqrt(lax.optimization_barrier(jnp.mean(branch * branch, axis=-1))) / jnp.sqrt(lax.optimization_barrier(jnp.mean(inputs * inputs, axis=-1)) + EPS_RATIO)
    return (inputs + branch, ratio_row)

def layer(inputs, segments, frozen, params):
    weight_in, weight_out, weight_expand, weight_reduce = frozen
    down_proj, down_bias, up_proj, up_bias, gain_rows, shifts = params
    row_count = inputs.shape[0]
    seq_count = row_count // SEQ_LEN
    qkv_all = low_back(low(matmul_high(low(inputs), weight_in)))
    qkv_all = qkv_all.reshape(seq_count, SEQ_LEN, 3, HEADS, HEAD_DIM)
    context = lax.map(jax.checkpoint(attend_one), (qkv_all[:, :, 0], qkv_all[:, :, 1], qkv_all[:, :, 2], segments.reshape(seq_count, SEQ_LEN)))
    context = low_back(low(context.reshape(row_count, D)))
    attended = low_back(matmul_high(context, weight_out))
    branch_one, ratio_one = adapter(attended, down_proj[0], down_bias[0], up_proj[0], up_bias[0])
    normed = layer_norm(inputs + branch_one, gain_rows[0], shifts[0])
    inner_act = low_back(matmul_high(low(normed), weight_expand))
    feed_out = low_back(matmul_high(low(gelu_exact(inner_act)), weight_reduce))
    branch_two, ratio_two = adapter(feed_out, down_proj[1], down_bias[1], up_proj[1], up_bias[1])
    output = layer_norm(normed + branch_two, gain_rows[1], shifts[1])
    return (output, jnp.stack([ratio_one, ratio_two]))

def reference(hidden_states, segment_ids, input_weight, output_weight, expand_weight, reduce_weight, adapter_down, adapter_down_bias, adapter_up, adapter_up_bias, norm_gain, norm_shift, output_grad):
    frozen = (input_weight.astype(jnp.float32), output_weight.astype(jnp.float32), expand_weight.astype(jnp.float32), reduce_weight.astype(jnp.float32))
    params = (adapter_down.astype(jnp.float32), adapter_down_bias, adapter_up.astype(jnp.float32), adapter_up_bias, norm_gain, norm_shift)
    group_rows = 8 * SEQ_LEN
    group_count = TOKENS // group_rows

    def one_group(running, group_data):
        grad_sum, ratio_sum, valid_sum = running
        inputs, segments, cotangent = group_data

        def forward(inputs_in, params_in):
            return layer(inputs_in, segments, frozen, params_in)
        output, pullback, ratios = jax.vjp(forward, inputs, params, has_aux=True)
        input_part, param_part = pullback(cotangent)
        valid_rows = (segments >= 0).astype(jnp.float32)
        grad_sum = jax.tree.map(lambda total, piece: total + piece, grad_sum, param_part)
        ratio_sum = ratio_sum + lax.optimization_barrier(jnp.sum(ratios * valid_rows[None, :], axis=1))
        valid_sum = valid_sum + jnp.sum(valid_rows)
        return ((grad_sum, ratio_sum, valid_sum), (output.astype(jnp.bfloat16), input_part))
    start = (jax.tree.map(jnp.zeros_like, params), jnp.zeros((2,), jnp.float32), jnp.zeros((), jnp.float32))
    stacked = (hidden_states.astype(jnp.float32).reshape(group_count, group_rows, D), segment_ids.reshape(group_count, group_rows), output_grad.astype(jnp.float32).reshape(group_count, group_rows, D))
    final_state, (outputs, input_parts) = lax.scan(one_group, start, stacked)
    grad_sum, ratio_sum, valid_sum = final_state
    return (outputs.reshape(TOKENS, D), input_parts.reshape(TOKENS, D), ratio_sum / valid_sum, grad_sum[0], grad_sum[1], grad_sum[2], grad_sum[3], grad_sum[4], grad_sum[5])
```

```python
import jax
import jax.numpy as jnp
from jax import lax
from jax.experimental import pallas as pl
from jax.experimental.pallas import tpu as pltpu
from jax.sharding import PartitionSpec as P

MESH = pl.DeviceIdType.MESH
PLANE = 4


def gather_kernel(depth, *refs):
    shards, outs = refs[:4], refs[4:8]
    own_sem, send_sem, recv_sem, pair_send, pair_recv = refs[8:]
    me = lax.axis_index("dp")
    core = lax.axis_index("head")
    z = me // PLANE
    step_a = 1 + core
    step_b = 2 - core
    a = (me // step_a) % 2
    b = (me // step_b) % 2
    peer_a = z * PLANE + (1 - a) * step_a + b * step_b
    peer_b = z * PLANE + a * step_a + (1 - b) * step_b
    up, down = me + PLANE, me - PLANE
    has_up, has_down = z < depth - 1, z > 0
    partner = 1 - core

    def owner(z_of, a_of, b_of):
        return z_of * PLANE + a_of * step_a + b_of * step_b

    barrier = pltpu.get_barrier_semaphore()

    def greet(cond, target):
        def signal():
            pl.semaphore_signal(barrier, inc=1, device_id=target, device_id_type=MESH)

        if cond is None:
            signal()
        else:
            pl.when(cond)(signal)

    greet(None, {"dp": peer_a})
    greet(None, {"dp": peer_b})
    greet(None, {"head": partner})
    greet(has_up, {"dp": up})
    greet(has_down, {"dp": down})
    pl.semaphore_wait(barrier, 3 + has_up.astype(jnp.int32) + has_down.astype(jnp.int32))

    pending = []

    def guarded(cond, act):
        if cond is None:
            act()
        else:
            pl.when(cond)(act)

    def send(cond, w, piece, src, dst, direction, slot, target):
        copy = pltpu.make_async_remote_copy(
            src_ref=src,
            dst_ref=dst,
            send_sem=send_sem.at[w, direction, slot],
            recv_sem=recv_sem.at[w, piece],
            device_id=target,
            device_id_type=MESH,
        )
        guarded(cond, copy.start)
        pending.append((cond, copy))

    def hand(cond, w, piece, view):
        copy = pltpu.make_async_remote_copy(
            src_ref=view,
            dst_ref=view,
            send_sem=pair_send.at[w, piece],
            recv_sem=pair_recv.at[w, piece],
            device_id={"head": partner},
            device_id_type=MESH,
        )
        guarded(cond, copy.start)
        pending.append((cond, copy))

    def both(x, y):
        return y if x is None else (x if y is None else jnp.logical_and(x, y))

    def view_of(w, piece):
        half = outs[w].shape[2] // 2
        return outs[w].at[piece, :, pl.ds(pl.multiple_of(core * half, 128), half)]

    def arrive(cond, w, piece):
        view = view_of(w, piece)

        def wait():
            pltpu.make_async_copy(view, view, recv_sem.at[w, piece]).wait()

        guarded(cond, wait)
        return view

    def start_own(w):
        half = outs[w].shape[2] // 2
        src = shards[w].at[:, pl.ds(pl.multiple_of(core * half, 128), half)]
        view = view_of(w, me)
        send(None, w, me, src, view, 0, 0, {"dp": peer_a})
        send(has_up, w, me, src, view, 1, 0, {"dp": up})
        send(has_down, w, me, src, view, 2, 0, {"dp": down})
        send(None, w, me, src, view, 3, 0, {"dp": peer_b})
        pltpu.make_async_copy(shards[w], outs[w].at[me], own_sem.at[w]).start()

    def first(w):
        piece = peer_a
        view = arrive(None, w, piece)
        send(has_up, w, piece, view, view, 1, 1, {"dp": up})
        send(has_down, w, piece, view, view, 2, 1, {"dp": down})
        send(None, w, piece, view, view, 3, 1, {"dp": peer_b})
        hand(None, w, piece, view)

    def line(w, dist):
        for k, a_of in enumerate((a, 1 - a)):
            slot = 2 * dist + k
            below = z >= dist
            piece = owner(z - dist, a_of, b)
            view = arrive(below, w, piece)
            send(both(below, has_up), w, piece, view, view, 1, slot, {"dp": up})
            send(below, w, piece, view, view, 3, slot, {"dp": peer_b})
            hand(below, w, piece, view)
            above = z + dist < depth
            piece = owner(z + dist, a_of, b)
            view = arrive(above, w, piece)
            send(both(above, has_down), w, piece, view, view, 2, slot, {"dp": down})
            send(above, w, piece, view, view, 3, 2 * depth + slot, {"dp": peer_b})
            hand(above, w, piece, view)

    def last(w):
        for z_of in range(depth):
            for a_of in range(2):
                piece = owner(z_of, a_of, 1 - b)
                view = arrive(None, w, piece)
                hand(None, w, piece, view)

    count = len(outs)
    for w in range(count):
        start_own(w)
        first(w)
        for dist in range(1, depth):
            line(w, dist)
            if w > 0 and dist == 1:
                last(w - 1)
    last(count - 1)

    for w in range(count):
        pltpu.make_async_copy(shards[w], outs[w].at[me], own_sem.at[w]).wait()
        half = outs[w].shape[2] // 2
        for z_of in range(depth):
            for a_of in range(2):
                for b_of in range(2):
                    piece = owner(z_of, a_of, b_of)
                    other = pl.ds(pl.multiple_of((1 - core) * half, 128), half)

                    def wait_pair(w=w, piece=piece, other=other):
                        view = outs[w].at[piece, :, other]
                        pltpu.make_async_copy(view, view, pair_recv.at[w, piece]).wait()

                    pl.when(piece != me)(wait_pair)
    for cond, copy in pending:
        guarded(cond, copy.wait_send)


def gather_weights(weights):
    size = lax.axis_size("dp")
    if size % PLANE or any(w.shape[0] % 16 or w.shape[1] % 256 for w in weights):
        return [lax.all_gather(w, "dp", axis=0, tiled=True) for w in weights]
    depth = size // PLANE
    count = len(weights)
    gathered = pl.pallas_call(
        lambda *refs: gather_kernel(depth, *refs),
        out_shape=[jax.ShapeDtypeStruct((size,) + w.shape, w.dtype) for w in weights],
        in_specs=[pl.BlockSpec(memory_space=pltpu.VMEM)] * count,
        out_specs=[pl.BlockSpec(memory_space=pl.ANY)] * count,
        scratch_shapes=[
            pltpu.SemaphoreType.DMA((count,)),
            pltpu.SemaphoreType.DMA((count, 4, 4 * depth)),
            pltpu.SemaphoreType.DMA((count, size)),
            pltpu.SemaphoreType.DMA((count, size)),
            pltpu.SemaphoreType.DMA((count, size)),
        ],
        compiler_params=pltpu.CompilerParams(collective_id=0, has_side_effects=True),
        name="gather_weights",
    )(*weights)
    return [g.reshape(size * w.shape[0], w.shape[1]) for g, w in zip(gathered, weights)]


HEAD_DIM = 64
SEQ_LEN = 512


EPS_NORM = 1e-12
EPS_RATIO = 1e-06
SCORE_SCALE = 0.125


def gelu_exact(values):
    return jax.nn.gelu(values, approximate=False)


def layer_norm(values, gain_row, shift_row):
    centred = values - jnp.mean(values, axis=-1, keepdims=True)
    variance = jnp.mean(centred * centred, axis=-1, keepdims=True)
    return centred * lax.rsqrt(variance + EPS_NORM) * gain_row + shift_row


def contract_rows(left_side, right_side):
    return lax.dot_general(
        left_side, right_side, (((0,), (0,)), ((), ())), preferred_element_type=jnp.float32
    )


def contract_last(left_side, right_side):
    return lax.dot_general(
        left_side, right_side, (((1,), (1,)), ((), ())), preferred_element_type=jnp.float32
    )


def mask_of(segment):
    positions = jnp.arange(segment.shape[0])
    return (segment[:, None] == segment[None, :]) & (segment[None, :] >= 0) | (
        positions[:, None] == positions[None, :]
    )


def attend_forward(seq_block):
    queries, key_rows, value_rows, segment = seq_block
    scores = (
        jnp.einsum("qhd,khd->hqk", queries, key_rows, preferred_element_type=jnp.float32)
        * SCORE_SCALE
    )
    scores = jnp.where(mask_of(segment)[None], scores, -1e30)
    row_max = jnp.max(scores, axis=-1, keepdims=True)
    exponents = jnp.exp(scores - row_max)
    row_total = jnp.sum(exponents, axis=-1, keepdims=True)
    attn_probs = (exponents / row_total).astype(jnp.bfloat16)
    context = jnp.einsum("hqk,khd->qhd", attn_probs, value_rows, preferred_element_type=jnp.float32)
    return (context.astype(jnp.bfloat16).reshape(SEQ_LEN, -1), row_max + jnp.log(row_total))


def attend_backward(seq_block):
    queries, key_rows, value_rows, segment, log_total, context_grad = seq_block
    scores = (
        jnp.einsum("qhd,khd->hqk", queries, key_rows, preferred_element_type=jnp.float32)
        * SCORE_SCALE
    )
    attn_probs = jnp.where(mask_of(segment)[None], jnp.exp(scores - log_total), 0.0)
    prob_grad = jnp.einsum(
        "qhd,khd->hqk", context_grad, value_rows, preferred_element_type=jnp.float32
    )
    score_grad = (
        attn_probs * (prob_grad - jnp.sum(attn_probs * prob_grad, axis=-1, keepdims=True))
    ).astype(jnp.bfloat16)
    query_grad = (
        jnp.einsum("hqk,khd->qhd", score_grad, key_rows, preferred_element_type=jnp.float32)
        * SCORE_SCALE
    )
    key_grad = (
        jnp.einsum("hqk,qhd->khd", score_grad, queries, preferred_element_type=jnp.float32)
        * SCORE_SCALE
    )
    value_grad = jnp.einsum(
        "hqk,qhd->khd",
        attn_probs.astype(jnp.bfloat16),
        context_grad,
        preferred_element_type=jnp.float32,
    )
    stacked = jnp.stack([query_grad, key_grad, value_grad], axis=1).astype(jnp.bfloat16)
    return stacked.reshape(SEQ_LEN, 3, -1)


def adapter_forward(inputs, down_proj, down_bias, up_proj, up_bias):
    inputs_low = inputs.astype(jnp.bfloat16)
    hidden = jnp.dot(inputs_low, down_proj, preferred_element_type=jnp.float32) + down_bias
    hidden_low = gelu_exact(hidden).astype(jnp.bfloat16)
    branch = jnp.dot(hidden_low, up_proj, preferred_element_type=jnp.float32) + up_bias
    ratio_row = jnp.sqrt(jnp.mean(branch * branch, axis=-1)) / jnp.sqrt(
        jnp.mean(inputs * inputs, axis=-1) + EPS_RATIO
    )
    return (inputs + branch, (inputs_low, hidden, hidden_low), ratio_row)


def adapter_backward(total_grad, kept_acts, down_proj, up_proj):
    inputs_low, hidden, hidden_low = kept_acts
    branch_grad = total_grad.astype(jnp.bfloat16)
    up_part = contract_rows(hidden_low, branch_grad)
    up_bias_part = jnp.sum(branch_grad.astype(jnp.float32), axis=0)
    _, gelu_pull = jax.vjp(gelu_exact, hidden)
    hidden_grad = gelu_pull(contract_last(branch_grad, up_proj))[0].astype(jnp.bfloat16)
    down_part = contract_rows(inputs_low, hidden_grad)
    down_bias_part = jnp.sum(hidden_grad.astype(jnp.float32), axis=0)
    input_part = (total_grad + contract_last(hidden_grad, down_proj)).astype(jnp.bfloat16)
    return (input_part, (down_part, down_bias_part, up_part, up_bias_part))


def tail(inputs, context, weight_out, weight_expand, weight_reduce, params):
    down_proj, down_bias, up_proj, up_bias, gain_rows, shifts = params
    attended = jnp.dot(context, weight_out, preferred_element_type=jnp.float32)
    branch_one, kept_one, ratio_one = adapter_forward(
        attended, down_proj[0], down_bias[0], up_proj[0], up_bias[0]
    )
    summed_one = inputs + branch_one
    normed = layer_norm(summed_one, gain_rows[0], shifts[0])
    inner_act = jnp.dot(
        normed.astype(jnp.bfloat16), weight_expand, preferred_element_type=jnp.float32
    )
    feed_out = jnp.dot(
        gelu_exact(inner_act).astype(jnp.bfloat16),
        weight_reduce,
        preferred_element_type=jnp.float32,
    )
    branch_two, kept_two, ratio_two = adapter_forward(
        feed_out, down_proj[1], down_bias[1], up_proj[1], up_bias[1]
    )
    summed_two = normed + branch_two
    output = layer_norm(summed_two, gain_rows[1], shifts[1])
    return (output, (summed_one, inner_act, summed_two, kept_one, kept_two), (ratio_one, ratio_two))


def body(
    hidden_states,
    segment_ids,
    input_weight,
    output_weight,
    expand_weight,
    reduce_weight,
    adapter_down,
    adapter_down_bias,
    adapter_up,
    adapter_up_bias,
    norm_gain,
    norm_shift,
    output_grad,
):
    row_count, model_width = hidden_states.shape
    heads = model_width // HEAD_DIM
    seq_count = row_count // SEQ_LEN
    params = (adapter_down, adapter_down_bias, adapter_up, adapter_up_bias, norm_gain, norm_shift)
    weight_in, weight_out, weight_expand, weight_reduce = gather_weights(
        [input_weight, output_weight, expand_weight, reduce_weight]
    )
    qkv_all = jnp.dot(hidden_states, weight_in, preferred_element_type=jnp.float32).astype(
        jnp.bfloat16
    )
    ids = segment_ids.reshape(seq_count, SEQ_LEN)
    split = qkv_all.reshape(seq_count, SEQ_LEN, 3, heads, HEAD_DIM)
    queries = split[:, :, 0]
    key_rows = split[:, :, 1]
    value_rows = split[:, :, 2]
    context, log_totals = lax.map(attend_forward, (queries, key_rows, value_rows, ids))
    context = context.reshape(row_count, model_width)
    inputs = hidden_states.astype(jnp.float32)
    output, saved_acts, ratios = tail(
        inputs, context, weight_out, weight_expand, weight_reduce, params
    )
    valid_rows = (segment_ids >= 0).astype(jnp.float32)
    ratio_sums = jnp.stack([jnp.sum(ratios[0] * valid_rows), jnp.sum(ratios[1] * valid_rows)])
    valid_count = jnp.sum(valid_rows)
    summed_one, inner_act, summed_two, kept_one, kept_two = saved_acts
    _, norm_pull_two = jax.vjp(layer_norm, summed_two, norm_gain[1], norm_shift[1])
    sum_two_grad, gain_two, shift_two = norm_pull_two(output_grad.astype(jnp.float32))
    feed_grad, parts_two = adapter_backward(sum_two_grad, kept_two, adapter_down[1], adapter_up[1])
    _, gelu_pull = jax.vjp(gelu_exact, inner_act)
    inner_grad = gelu_pull(contract_last(feed_grad, weight_reduce))[0].astype(jnp.bfloat16)
    normed_grad = sum_two_grad + contract_last(inner_grad, weight_expand)
    _, norm_pull_one = jax.vjp(layer_norm, summed_one, norm_gain[0], norm_shift[0])
    sum_one_grad, gain_one, shift_one = norm_pull_one(normed_grad)
    attended_grad, parts_one = adapter_backward(
        sum_one_grad, kept_one, adapter_down[0], adapter_up[0]
    )
    context_grad = contract_last(attended_grad, weight_out).astype(jnp.bfloat16)
    context_grad = context_grad.reshape(seq_count, SEQ_LEN, heads, HEAD_DIM)
    qkv_grad = lax.map(
        attend_backward, (queries, key_rows, value_rows, ids, log_totals, context_grad)
    )
    qkv_grad = qkv_grad.reshape(row_count, 3 * model_width)
    input_grad = sum_one_grad + contract_last(qkv_grad, weight_in)
    local_sums = (
        jnp.stack([parts_one[0], parts_two[0]]),
        jnp.stack([parts_one[1], parts_two[1]]),
        jnp.stack([parts_one[2], parts_two[2]]),
        jnp.stack([parts_one[3], parts_two[3]]),
        jnp.stack([gain_one, gain_two]),
        jnp.stack([shift_one, shift_two]),
        ratio_sums,
        valid_count,
    )
    (
        down_grad,
        down_bias_grad,
        up_grad,
        up_bias_grad,
        gain_grad,
        shift_grad,
        ratio_total,
        count_total,
    ) = lax.psum(
        (
            local_sums[0],
            local_sums[1],
            local_sums[2],
            local_sums[3],
            local_sums[4],
            local_sums[5],
            local_sums[6],
            local_sums[7],
        ),
        ("dp", "head"),
    )
    return (
        output.astype(jnp.bfloat16),
        input_grad,
        ratio_total / count_total,
        down_grad,
        down_bias_grad,
        up_grad,
        up_bias_grad,
        gain_grad,
        shift_grad,
    )


def solution(mesh):
    in_specs = (
        P(("dp", "head"), None),
        P(("dp", "head")),
        P("dp", None),
        P("dp", None),
        P("dp", None),
        P("dp", None),
        P(),
        P(),
        P(),
        P(),
        P(),
        P(),
        P(("dp", "head"), None),
    )
    out_specs = (
        P(("dp", "head"), None),
        P(("dp", "head"), None),
        P(),
        P(),
        P(),
        P(),
        P(),
        P(),
        P(),
    )
    return jax.shard_map(body, mesh=mesh, in_specs=in_specs, out_specs=out_specs, check_vma=False)
```

```python
import jax
import jax.numpy as jnp
from jax import lax
from jax.experimental import pallas as pl
from jax.experimental.pallas import tpu as pltpu
from jax.sharding import PartitionSpec as P

MESH = pl.DeviceIdType.MESH
PLANE = 4


def gather_kernel(depth, *refs):
    shards, outs = refs[:4], refs[4:8]
    own_sem, send_sem, recv_sem, pair_send, pair_recv = refs[8:]
    me = lax.axis_index("dp")
    core = lax.axis_index("head")
    z = me // PLANE
    step_a = 1 + core
    step_b = 2 - core
    a = (me // step_a) % 2
    b = (me // step_b) % 2
    peer_a = z * PLANE + (1 - a) * step_a + b * step_b
    peer_b = z * PLANE + a * step_a + (1 - b) * step_b
    up, down = me + PLANE, me - PLANE
    has_up, has_down = z < depth - 1, z > 0
    partner = 1 - core

    def owner(z_of, a_of, b_of):
        return z_of * PLANE + a_of * step_a + b_of * step_b

    barrier = pltpu.get_barrier_semaphore()

    def greet(cond, target):
        def signal():
            pl.semaphore_signal(barrier, inc=1, device_id=target, device_id_type=MESH)

        if cond is None:
            signal()
        else:
            pl.when(cond)(signal)

    greet(None, {"dp": peer_a})
    greet(None, {"dp": peer_b})
    greet(None, {"head": partner})
    greet(has_up, {"dp": up})
    greet(has_down, {"dp": down})
    pl.semaphore_wait(barrier, 3 + has_up.astype(jnp.int32) + has_down.astype(jnp.int32))

    pending = []

    def guarded(cond, act):
        if cond is None:
            act()
        else:
            pl.when(cond)(act)

    def send(cond, w, piece, src, dst, direction, slot, target):
        copy = pltpu.make_async_remote_copy(
            src_ref=src,
            dst_ref=dst,
            send_sem=send_sem.at[w, direction, slot],
            recv_sem=recv_sem.at[w, piece],
            device_id=target,
            device_id_type=MESH,
        )
        guarded(cond, copy.start)
        pending.append((cond, copy))

    def hand(cond, w, piece, view):
        copy = pltpu.make_async_remote_copy(
            src_ref=view,
            dst_ref=view,
            send_sem=pair_send.at[w, piece],
            recv_sem=pair_recv.at[w, piece],
            device_id={"head": partner},
            device_id_type=MESH,
        )
        guarded(cond, copy.start)
        pending.append((cond, copy))

    def both(x, y):
        return y if x is None else (x if y is None else jnp.logical_and(x, y))

    def view_of(w, piece):
        half = outs[w].shape[2] // 2
        return outs[w].at[piece, :, pl.ds(pl.multiple_of(core * half, 128), half)]

    def arrive(cond, w, piece):
        view = view_of(w, piece)

        def wait():
            pltpu.make_async_copy(view, view, recv_sem.at[w, piece]).wait()

        guarded(cond, wait)
        return view

    def start_own(w):
        half = outs[w].shape[2] // 2
        src = shards[w].at[:, pl.ds(pl.multiple_of(core * half, 128), half)]
        view = view_of(w, me)
        send(None, w, me, src, view, 0, 0, {"dp": peer_a})
        send(has_up, w, me, src, view, 1, 0, {"dp": up})
        send(has_down, w, me, src, view, 2, 0, {"dp": down})
        send(None, w, me, src, view, 3, 0, {"dp": peer_b})
        pltpu.make_async_copy(shards[w], outs[w].at[me], own_sem.at[w]).start()

    def first(w):
        piece = peer_a
        view = arrive(None, w, piece)
        send(has_up, w, piece, view, view, 1, 1, {"dp": up})
        send(has_down, w, piece, view, view, 2, 1, {"dp": down})
        send(None, w, piece, view, view, 3, 1, {"dp": peer_b})
        hand(None, w, piece, view)

    def line(w, dist):
        for k, a_of in enumerate((a, 1 - a)):
            slot = 2 * dist + k
            below = z >= dist
            piece = owner(z - dist, a_of, b)
            view = arrive(below, w, piece)
            send(both(below, has_up), w, piece, view, view, 1, slot, {"dp": up})
            send(below, w, piece, view, view, 3, slot, {"dp": peer_b})
            hand(below, w, piece, view)
            above = z + dist < depth
            piece = owner(z + dist, a_of, b)
            view = arrive(above, w, piece)
            send(both(above, has_down), w, piece, view, view, 2, slot, {"dp": down})
            send(above, w, piece, view, view, 3, 2 * depth + slot, {"dp": peer_b})
            hand(above, w, piece, view)

    def last(w):
        for z_of in range(depth):
            for a_of in range(2):
                piece = owner(z_of, a_of, 1 - b)
                view = arrive(None, w, piece)
                hand(None, w, piece, view)

    count = len(outs)
    for w in range(count):
        start_own(w)
        first(w)
        for dist in range(1, depth):
            line(w, dist)
            if w > 0 and dist == 1:
                last(w - 1)
    last(count - 1)

    for w in range(count):
        pltpu.make_async_copy(shards[w], outs[w].at[me], own_sem.at[w]).wait()
        half = outs[w].shape[2] // 2
        for z_of in range(depth):
            for a_of in range(2):
                for b_of in range(2):
                    piece = owner(z_of, a_of, b_of)
                    other = pl.ds(pl.multiple_of((1 - core) * half, 128), half)

                    def wait_pair(w=w, piece=piece, other=other):
                        view = outs[w].at[piece, :, other]
                        pltpu.make_async_copy(view, view, pair_recv.at[w, piece]).wait()

                    pl.when(piece != me)(wait_pair)
    for cond, copy in pending:
        guarded(cond, copy.wait_send)


def gather_weights(weights):
    size = lax.axis_size("dp")
    if size % PLANE or any(w.shape[0] % 16 or w.shape[1] % 256 for w in weights):
        return [lax.all_gather(w, "dp", axis=0, tiled=True) for w in weights]
    depth = size // PLANE
    count = len(weights)
    gathered = pl.pallas_call(
        lambda *refs: gather_kernel(depth, *refs),
        out_shape=[jax.ShapeDtypeStruct((size,) + w.shape, w.dtype) for w in weights],
        in_specs=[pl.BlockSpec(memory_space=pltpu.VMEM)] * count,
        out_specs=[pl.BlockSpec(memory_space=pl.ANY)] * count,
        scratch_shapes=[
            pltpu.SemaphoreType.DMA((count,)),
            pltpu.SemaphoreType.DMA((count, 4, 4 * depth)),
            pltpu.SemaphoreType.DMA((count, size)),
            pltpu.SemaphoreType.DMA((count, size)),
            pltpu.SemaphoreType.DMA((count, size)),
        ],
        compiler_params=pltpu.CompilerParams(collective_id=0, has_side_effects=True),
        name="gather_weights",
    )(*weights)
    return [g.reshape(size * w.shape[0], w.shape[1]) for g, w in zip(gathered, weights)]


HEAD_DIM = 64
SEQ_LEN = 512
PAIR = 2 * HEAD_DIM
LOG2E = 1.4426950408889634
EPS_NORM = 1e-12
EPS_RATIO = 1e-06
SCORE_SCALE = 0.125
VMEM_LIMIT = 60 * 1024 * 1024

TAIL_POLY = (
    0.09973556672,
    0.09973643158,
    0.09346635627,
    0.08160309818,
    0.05897520771,
    0.06369893559,
    -0.03171721207,
    0.0955967654,
    -0.08087713545,
    0.01978196913,
)
INV_SQRT_2PI = 0.3989422804014327


def gelu_pair(x):
    t = 1.0 / (1.0 + 0.25 * jnp.abs(x))
    poly = jnp.full_like(t, TAIL_POLY[-1])
    for coef in TAIL_POLY[-2::-1]:
        poly = poly * t + coef
    bell = jnp.exp2(x * x * (-0.5 * LOG2E))
    below = bell * (t * poly)
    cdf = jnp.where(x >= 0, 1.0 - below, below)
    return x * cdf, cdf + x * (bell * INV_SQRT_2PI)


def dot(a, b):
    return jnp.dot(a, b, preferred_element_type=jnp.float32)


def dot_nt(a, b):
    return lax.dot_general(a, b, (((1,), (1,)), ((), ())), preferred_element_type=jnp.float32)


def dot_tn(a, b):
    return lax.dot_general(a, b, (((0,), (0,)), ((), ())), preferred_element_type=jnp.float32)


def score_bias(seg_row):
    across = jnp.broadcast_to(seg_row, (SEQ_LEN, SEQ_LEN))
    tall = jnp.broadcast_to(seg_row, (PAIR, SEQ_LEN)).T
    along = jnp.concatenate([tall] * (SEQ_LEN // PAIR), axis=1)
    row = lax.broadcasted_iota(jnp.int32, (SEQ_LEN, SEQ_LEN), 0)
    col = lax.broadcasted_iota(jnp.int32, (SEQ_LEN, SEQ_LEN), 1)
    allowed = ((across == along) & (across >= 0)) | (row == col)
    return jnp.where(allowed, 0.0, -1e30)


def head_lanes():
    lane = lax.broadcasted_iota(jnp.int32, (1, PAIR), 1)
    first = (lane < HEAD_DIM).astype(jnp.float32)
    return lane < HEAD_DIM, (first.astype(jnp.bfloat16), (1.0 - first).astype(jnp.bfloat16))


def cols(start, width):
    return pl.ds(pl.multiple_of(start, 128), width)


def attend_kernel(width, hid_ref, seg_ref, w_ref, qkv_ref, ctx_ref, bias_ref):
    step = 256

    def project(c, _):
        at = cols(c * step, step)
        qkv_ref[:, at] = dot(hid_ref[...], w_ref[:, at]).astype(jnp.bfloat16)
        return 0

    lax.fori_loop(0, 3 * width // step, project, 0)
    bias_ref[...] = score_bias(seg_ref[0])
    low, masks = head_lanes()

    def pair(h, _):
        q = qkv_ref[:, cols(h * PAIR, PAIR)]
        k = qkv_ref[:, cols(width + h * PAIR, PAIR)]
        v = qkv_ref[:, cols(2 * width + h * PAIR, PAIR)]
        v_ones = jnp.concatenate([v, jnp.ones_like(v)], axis=1)
        parts = []
        for mask in masks:
            s = dot_nt(q * mask, k) * (SCORE_SCALE * LOG2E) + bias_ref[...]
            e = jnp.exp2(s - jnp.max(s, axis=1, keepdims=True)).astype(jnp.bfloat16)
            o = dot(e, v_ones)
            parts.append(o[:, :PAIR] / o[:, PAIR:])
        ctx_ref[:, cols(h * PAIR, PAIR)] = jnp.where(low, parts[0], parts[1]).astype(jnp.bfloat16)
        return 0

    lax.fori_loop(0, width // PAIR, pair, 0)


def attend_forward(hidden, seg_rows, weight_in):
    rows, width = hidden.shape
    seqs = rows // SEQ_LEN
    return pl.pallas_call(
        lambda *refs: attend_kernel(width, *refs),
        grid=(seqs,),
        out_shape=[
            jax.ShapeDtypeStruct((rows, 3 * width), jnp.bfloat16),
            jax.ShapeDtypeStruct((rows, width), jnp.bfloat16),
        ],
        in_specs=[
            pl.BlockSpec((SEQ_LEN, width), lambda i: (i, 0)),
            pl.BlockSpec((1, 1, SEQ_LEN), lambda i: (i, 0, 0)),
            pl.BlockSpec((width, 3 * width), lambda i: (0, 0)),
        ],
        out_specs=[
            pl.BlockSpec((SEQ_LEN, 3 * width), lambda i: (i, 0)),
            pl.BlockSpec((SEQ_LEN, width), lambda i: (i, 0)),
        ],
        scratch_shapes=[pltpu.VMEM((SEQ_LEN, SEQ_LEN), jnp.float32)],
        compiler_params=pltpu.CompilerParams(vmem_limit_bytes=VMEM_LIMIT),
        cost_estimate=pl.CostEstimate(
            flops=rows * width * (6 * width + 4 * SEQ_LEN),
            bytes_accessed=2 * rows * 5 * width + 6 * width * width,
            transcendentals=rows * SEQ_LEN * width // HEAD_DIM,
        ),
        name="attend_forward",
    )(hidden, seg_rows, weight_in)


def attend_grad_kernel(width, qkv_ref, cg_ref, seg_ref, sog_ref, w_ref, out_ref, grad_ref, bias_ref):
    bias_ref[...] = score_bias(seg_ref[0])
    low, masks = head_lanes()

    def pair(h, _):
        q = qkv_ref[:, cols(h * PAIR, PAIR)]
        k = qkv_ref[:, cols(width + h * PAIR, PAIR)]
        v = qkv_ref[:, cols(2 * width + h * PAIR, PAIR)]
        g = cg_ref[:, cols(h * PAIR, PAIR)]
        parts = []
        for mask in masks:
            s = dot_nt(k * mask, q) * (SCORE_SCALE * LOG2E) + bias_ref[...]
            e = jnp.exp2(s - jnp.max(s, axis=0, keepdims=True))
            p = e * (1.0 / jnp.sum(e, axis=0, keepdims=True))
            pg = dot_nt(v * mask, g)
            ds = (p * (pg - jnp.sum(p * pg, axis=0, keepdims=True))).astype(jnp.bfloat16)
            parts.append((dot_tn(ds, k), dot(ds, q), dot(p.astype(jnp.bfloat16), g)))
        for n, scale in enumerate((SCORE_SCALE, SCORE_SCALE, 1.0)):
            both = jnp.where(low, parts[0][n], parts[1][n]) * scale
            grad_ref[:, cols(n * width + h * PAIR, PAIR)] = both.astype(jnp.bfloat16)
        return 0

    lax.fori_loop(0, width // PAIR, pair, 0)
    step = 256

    def back(c, _):
        at = cols(c * step, step)
        out_ref[:, at] = sog_ref[:, at] + dot_nt(grad_ref[...], w_ref[at, :])
        return 0

    lax.fori_loop(0, width // step, back, 0)


def attend_backward(qkv, ctx_grad, seg_rows, sum_one_grad, weight_in):
    rows, width = ctx_grad.shape
    return pl.pallas_call(
        lambda *refs: attend_grad_kernel(width, *refs),
        grid=(rows // SEQ_LEN,),
        out_shape=jax.ShapeDtypeStruct((rows, width), jnp.float32),
        in_specs=[
            pl.BlockSpec((SEQ_LEN, 3 * width), lambda i: (i, 0)),
            pl.BlockSpec((SEQ_LEN, width), lambda i: (i, 0)),
            pl.BlockSpec((1, 1, SEQ_LEN), lambda i: (i, 0, 0)),
            pl.BlockSpec((SEQ_LEN, width), lambda i: (i, 0)),
            pl.BlockSpec((width, 3 * width), lambda i: (0, 0)),
        ],
        out_specs=pl.BlockSpec((SEQ_LEN, width), lambda i: (i, 0)),
        scratch_shapes=[
            pltpu.VMEM((SEQ_LEN, 3 * width), jnp.bfloat16),
            pltpu.VMEM((SEQ_LEN, SEQ_LEN), jnp.float32),
        ],
        compiler_params=pltpu.CompilerParams(vmem_limit_bytes=VMEM_LIMIT),
        cost_estimate=pl.CostEstimate(
            flops=rows * width * (6 * width + 10 * SEQ_LEN),
            bytes_accessed=2 * rows * 8 * width + 6 * width * width,
            transcendentals=rows * SEQ_LEN * width // HEAD_DIM,
        ),
        name="attend_backward",
    )(qkv, ctx_grad, seg_rows, sum_one_grad, weight_in)


def row_mean(x):
    return jnp.mean(x, axis=-1, keepdims=True)


def col_sum(x):
    return jnp.sum(x, axis=0, keepdims=True)


def layer_norm(u, gain, shift):
    centred = u - row_mean(u)
    scale = lax.rsqrt(row_mean(centred * centred) + EPS_NORM)
    hat = centred * scale
    return hat, scale, hat * gain + shift


def layer_norm_grad(hat, scale, gain, grad):
    gg = grad * gain
    return scale * (gg - row_mean(gg) - hat * row_mean(gg * hat))


def middle_kernel(
    ff,
    chunk,
    ctx_ref,
    hid_ref,
    og_ref,
    seg_ref,
    wo_ref,
    we_ref,
    wr_ref,
    down_ref,
    down_bias_ref,
    up_ref,
    up_bias_ref,
    gain_ref,
    shift_ref,
    out_ref,
    sog_ref,
    cg_ref,
    sums_ref,
    slope_ref,
    normed_ref,
    acc_ref,
):
    rank = up_ref.shape[1]
    small = 4 * rank

    @pl.when(pl.program_id(0) == 0)
    def _():
        sums_ref[...] = jnp.zeros_like(sums_ref)

    def adapter(k, a):
        a_low = a.astype(jnp.bfloat16)
        act, slope = gelu_pair(dot(a_low, down_ref[k]) + down_bias_ref[k : k + 1, :])
        act = act.astype(jnp.bfloat16)
        branch = dot(act, up_ref[k]) + up_bias_ref[k : k + 1, :]
        ratio = jnp.sqrt(row_mean(branch * branch)) / jnp.sqrt(row_mean(a * a) + EPS_RATIO)
        return branch, ratio, (a_low, act, slope)

    def add(row, value):
        sums_ref[row : row + 1, : value.shape[1]] += value

    def adapter_grad(k, kept, grad):
        a_low, act, slope = kept
        grad_low = grad.astype(jnp.bfloat16)
        hidden_grad = slope * dot_nt(grad_low, up_ref[k])
        hidden_grad = hidden_grad.astype(jnp.bfloat16)
        sums_ref[k * rank : (k + 1) * rank, :] += dot_tn(hidden_grad, a_low)
        sums_ref[(2 + k) * rank : (3 + k) * rank, :] += dot_tn(act, grad_low)
        add(small + k, col_sum(grad_low.astype(jnp.float32)))
        add(small + 6 + k, col_sum(hidden_grad.astype(jnp.float32)))
        return (grad + dot_nt(hidden_grad, down_ref[k])).astype(jnp.bfloat16)

    gain_one, gain_two = gain_ref[0:1, :], gain_ref[1:2, :]
    attended = dot(ctx_ref[...], wo_ref[...])
    branch, ratio_one, kept_one = adapter(0, attended)
    hat_one, scale_one, normed = layer_norm(
        hid_ref[...].astype(jnp.float32) + attended + branch, gain_one, shift_ref[0:1, :]
    )
    normed_ref[...] = normed.astype(jnp.bfloat16)
    acc_ref[...] = jnp.zeros_like(acc_ref)

    def feed(c, _):
        at = cols(c * chunk, chunk)
        act, slope = gelu_pair(dot(normed_ref[...], we_ref[:, at]))
        slope_ref[:, at] = slope
        acc_ref[...] += dot(act.astype(jnp.bfloat16), wr_ref[at, :])
        return 0

    lax.fori_loop(0, ff // chunk, feed, 0, unroll=2)
    feed_out = acc_ref[...]
    branch, ratio_two, kept_two = adapter(1, feed_out)
    hat_two, scale_two, final = layer_norm(normed + feed_out + branch, gain_two, shift_ref[1:2, :])
    out_ref[...] = final.astype(jnp.bfloat16)

    lane = lax.broadcasted_iota(jnp.int32, (1, 128), 1)
    ratios = jnp.where(lane == 0, ratio_one, jnp.where(lane == 1, ratio_two, 1.0))
    valid = (seg_ref[0] >= 0).astype(jnp.float32)
    stats = jnp.dot(
        jnp.broadcast_to(valid, (8, valid.shape[1])),
        ratios,
        precision=lax.Precision.HIGHEST,
        preferred_element_type=jnp.float32,
    )
    add(small + 8, stats[0:1, :])

    grad = og_ref[...].astype(jnp.float32)
    add(small + 3, col_sum(grad * hat_two))
    add(small + 5, col_sum(grad))
    sum_two_grad = layer_norm_grad(hat_two, scale_two, gain_two, grad)
    normed_ref[...] = adapter_grad(1, kept_two, sum_two_grad)
    acc_ref[...] = sum_two_grad

    def feed_grad(c, _):
        at = cols(c * chunk, chunk)
        inner_grad = slope_ref[:, at] * dot_nt(normed_ref[...], wr_ref[at, :])
        acc_ref[...] += dot_nt(inner_grad.astype(jnp.bfloat16), we_ref[:, at])
        return 0

    lax.fori_loop(0, ff // chunk, feed_grad, 0, unroll=2)
    grad = acc_ref[...]
    add(small + 2, col_sum(grad * hat_one))
    add(small + 4, col_sum(grad))
    sum_one_grad = layer_norm_grad(hat_one, scale_one, gain_one, grad)
    sog_ref[...] = sum_one_grad
    attended_grad = adapter_grad(0, kept_one, sum_one_grad)
    cg_ref[...] = dot_nt(attended_grad, wo_ref[...]).astype(jnp.bfloat16)


TILE = 256
CHUNK = 512
SUM_ROWS = 288


def middle(ctx, hidden, output_grad, seg_ids, frozen, params):
    rows, width = hidden.shape
    weight_out, weight_expand, weight_reduce = frozen
    ff = weight_expand.shape[1]
    seg_tiles = seg_ids.reshape(rows // TILE, 1, TILE)
    whole = [weight_out, weight_expand, weight_reduce, *params]

    def tile_spec(n):
        return pl.BlockSpec((TILE, n), lambda i: (i, 0))

    def whole_spec(x):
        return pl.BlockSpec(x.shape, lambda i: (0,) * x.ndim, pipeline_mode=pl.Buffered(1))

    return pl.pallas_call(
        lambda *refs: middle_kernel(ff, CHUNK, *refs),
        grid=(rows // TILE,),
        out_shape=[
            jax.ShapeDtypeStruct((rows, width), jnp.bfloat16),
            jax.ShapeDtypeStruct((rows, width), jnp.float32),
            jax.ShapeDtypeStruct((rows, width), jnp.bfloat16),
            jax.ShapeDtypeStruct((SUM_ROWS, width), jnp.float32),
        ],
        in_specs=[tile_spec(width)] * 3
        + [pl.BlockSpec((1, 1, TILE), lambda i: (i, 0, 0))]
        + [whole_spec(x) for x in whole],
        out_specs=[tile_spec(width)] * 3 + [pl.BlockSpec((SUM_ROWS, width), lambda i: (0, 0))],
        scratch_shapes=[
            pltpu.VMEM((TILE, ff), jnp.float32),
            pltpu.VMEM((TILE, width), jnp.bfloat16),
            pltpu.VMEM((TILE, width), jnp.float32),
        ],
        compiler_params=pltpu.CompilerParams(vmem_limit_bytes=VMEM_LIMIT),
        cost_estimate=pl.CostEstimate(
            flops=4 * rows * width * (width + 2 * ff),
            bytes_accessed=14 * rows * width + 2 * width * (width + 2 * ff),
            transcendentals=2 * rows * ff,
        ),
        name="middle",
    )(ctx, hidden, output_grad, seg_tiles, *whole)


def body(
    hidden_states,
    segment_ids,
    input_weight,
    output_weight,
    expand_weight,
    reduce_weight,
    adapter_down,
    adapter_down_bias,
    adapter_up,
    adapter_up_bias,
    norm_gain,
    norm_shift,
    output_grad,
):
    weight_in, *frozen = gather_weights(
        [input_weight, output_weight, expand_weight, reduce_weight]
    )
    rank = adapter_up.shape[1]
    seg_rows = segment_ids.reshape(-1, 1, SEQ_LEN)
    qkv, ctx = attend_forward(hidden_states, seg_rows, weight_in)
    params = (
        adapter_down,
        adapter_down_bias,
        adapter_up,
        adapter_up_bias,
        norm_gain,
        norm_shift,
    )
    output, sum_one_grad, ctx_grad, sums = middle(
        ctx, hidden_states, output_grad, segment_ids, frozen, params
    )
    sums = lax.psum(sums, ("dp", "head"))
    input_grad = attend_backward(qkv, ctx_grad, seg_rows, sum_one_grad, weight_in)
    small = 4 * rank
    stats = sums[small + 8]
    return (
        output,
        input_grad,
        stats[:2] / stats[2],
        jnp.transpose(sums[: 2 * rank].reshape(2, rank, -1), (0, 2, 1)),
        sums[small + 6 : small + 8, :rank],
        sums[2 * rank : small].reshape(2, rank, -1),
        sums[small : small + 2],
        sums[small + 2 : small + 4],
        sums[small + 4 : small + 6],
    )


def solution(mesh):
    tokens = P(("dp", "head"), None)
    in_specs = (tokens, P(("dp", "head"))) + (P("dp", None),) * 4 + (P(),) * 6 + (tokens,)
    out_specs = (tokens, tokens) + (P(),) * 7
    return jax.shard_map(body, mesh=mesh, in_specs=in_specs, out_specs=out_specs, check_vma=False)
```

```python
import jax
import jax.numpy as jnp
from jax import lax
from jax.experimental import pallas as pl
from jax.experimental.pallas import tpu as pltpu
from jax.sharding import PartitionSpec as P

MESH = pl.DeviceIdType.MESH
PLANE = 4


def gather_kernel(depth, *refs):
    shards, outs = refs[:4], refs[4:8]
    own_sem, send_sem, recv_sem, pair_send, pair_recv = refs[8:]
    me = lax.axis_index("dp")
    core = lax.axis_index("head")
    z = me // PLANE
    step_a = 1 + core
    step_b = 2 - core
    a = (me // step_a) % 2
    b = (me // step_b) % 2
    peer_a = z * PLANE + (1 - a) * step_a + b * step_b
    peer_b = z * PLANE + a * step_a + (1 - b) * step_b
    up, down = me + PLANE, me - PLANE
    has_up, has_down = z < depth - 1, z > 0
    partner = 1 - core

    def owner(z_of, a_of, b_of):
        return z_of * PLANE + a_of * step_a + b_of * step_b

    barrier = pltpu.get_barrier_semaphore()

    def greet(cond, target):
        def signal():
            pl.semaphore_signal(barrier, inc=1, device_id=target, device_id_type=MESH)

        if cond is None:
            signal()
        else:
            pl.when(cond)(signal)

    greet(None, {"dp": peer_a})
    greet(None, {"dp": peer_b})
    greet(None, {"head": partner})
    greet(has_up, {"dp": up})
    greet(has_down, {"dp": down})
    pl.semaphore_wait(barrier, 3 + has_up.astype(jnp.int32) + has_down.astype(jnp.int32))

    pending = []

    def guarded(cond, act):
        if cond is None:
            act()
        else:
            pl.when(cond)(act)

    def send(cond, w, piece, src, dst, direction, slot, target):
        copy = pltpu.make_async_remote_copy(
            src_ref=src,
            dst_ref=dst,
            send_sem=send_sem.at[w, direction, slot],
            recv_sem=recv_sem.at[w, piece],
            device_id=target,
            device_id_type=MESH,
        )
        guarded(cond, copy.start)
        pending.append((cond, copy))

    def hand(cond, w, piece, view):
        copy = pltpu.make_async_remote_copy(
            src_ref=view,
            dst_ref=view,
            send_sem=pair_send.at[w, piece],
            recv_sem=pair_recv.at[w, piece],
            device_id={"head": partner},
            device_id_type=MESH,
        )
        guarded(cond, copy.start)
        pending.append((cond, copy))

    def both(x, y):
        return y if x is None else (x if y is None else jnp.logical_and(x, y))

    def view_of(w, piece):
        half = outs[w].shape[2] // 2
        return outs[w].at[piece, :, pl.ds(pl.multiple_of(core * half, 128), half)]

    def arrive(cond, w, piece):
        view = view_of(w, piece)

        def wait():
            pltpu.make_async_copy(view, view, recv_sem.at[w, piece]).wait()

        guarded(cond, wait)
        return view

    def start_own(w):
        half = outs[w].shape[2] // 2
        src = shards[w].at[:, pl.ds(pl.multiple_of(core * half, 128), half)]
        view = view_of(w, me)
        send(None, w, me, src, view, 0, 0, {"dp": peer_a})
        send(has_up, w, me, src, view, 1, 0, {"dp": up})
        send(has_down, w, me, src, view, 2, 0, {"dp": down})
        send(None, w, me, src, view, 3, 0, {"dp": peer_b})
        pltpu.make_async_copy(shards[w], outs[w].at[me], own_sem.at[w]).start()

    def first(w):
        piece = peer_a
        view = arrive(None, w, piece)
        send(has_up, w, piece, view, view, 1, 1, {"dp": up})
        send(has_down, w, piece, view, view, 2, 1, {"dp": down})
        send(None, w, piece, view, view, 3, 1, {"dp": peer_b})
        hand(None, w, piece, view)

    def line(w, dist):
        for k, a_of in enumerate((a, 1 - a)):
            slot = 2 * dist + k
            below = z >= dist
            piece = owner(z - dist, a_of, b)
            view = arrive(below, w, piece)
            send(both(below, has_up), w, piece, view, view, 1, slot, {"dp": up})
            send(below, w, piece, view, view, 3, slot, {"dp": peer_b})
            hand(below, w, piece, view)
            above = z + dist < depth
            piece = owner(z + dist, a_of, b)
            view = arrive(above, w, piece)
            send(both(above, has_down), w, piece, view, view, 2, slot, {"dp": down})
            send(above, w, piece, view, view, 3, 2 * depth + slot, {"dp": peer_b})
            hand(above, w, piece, view)

    def last(w):
        for z_of in range(depth):
            for a_of in range(2):
                piece = owner(z_of, a_of, 1 - b)
                view = arrive(None, w, piece)
                hand(None, w, piece, view)

    count = len(outs)
    for w in range(count):
        start_own(w)
        first(w)
        for dist in range(1, depth):
            line(w, dist)
            if w > 0 and dist == 1:
                last(w - 1)
    last(count - 1)

    for w in range(count):
        pltpu.make_async_copy(shards[w], outs[w].at[me], own_sem.at[w]).wait()
        half = outs[w].shape[2] // 2
        for z_of in range(depth):
            for a_of in range(2):
                for b_of in range(2):
                    piece = owner(z_of, a_of, b_of)
                    other = pl.ds(pl.multiple_of((1 - core) * half, 128), half)

                    def wait_pair(w=w, piece=piece, other=other):
                        view = outs[w].at[piece, :, other]
                        pltpu.make_async_copy(view, view, pair_recv.at[w, piece]).wait()

                    pl.when(piece != me)(wait_pair)
    for cond, copy in pending:
        guarded(cond, copy.wait_send)


def gather_weights(weights):
    size = lax.axis_size("dp")
    if size % PLANE or any(w.shape[0] % 16 or w.shape[1] % 256 for w in weights):
        return [lax.all_gather(w, "dp", axis=0, tiled=True) for w in weights]
    depth = size // PLANE
    count = len(weights)
    gathered = pl.pallas_call(
        lambda *refs: gather_kernel(depth, *refs),
        out_shape=[jax.ShapeDtypeStruct((size,) + w.shape, w.dtype) for w in weights],
        in_specs=[pl.BlockSpec(memory_space=pltpu.VMEM)] * count,
        out_specs=[pl.BlockSpec(memory_space=pl.ANY)] * count,
        scratch_shapes=[
            pltpu.SemaphoreType.DMA((count,)),
            pltpu.SemaphoreType.DMA((count, 4, 4 * depth)),
            pltpu.SemaphoreType.DMA((count, size)),
            pltpu.SemaphoreType.DMA((count, size)),
            pltpu.SemaphoreType.DMA((count, size)),
        ],
        compiler_params=pltpu.CompilerParams(collective_id=0, has_side_effects=True),
        name="gather_weights",
    )(*weights)
    return [g.reshape(size * w.shape[0], w.shape[1]) for g, w in zip(gathered, weights)]


HEAD_DIM = 64
SEQ_LEN = 512
PAIR = 2 * HEAD_DIM
LOG2E = 1.4426950408889634
EPS_NORM = 1e-12
EPS_RATIO = 1e-06
SCORE_SCALE = 0.125
VMEM_LIMIT = 60 * 1024 * 1024

TAIL_POLY = (
    0.09973556672,
    0.09973643158,
    0.09346635627,
    0.08160309818,
    0.05897520771,
    0.06369893559,
    -0.03171721207,
    0.0955967654,
    -0.08087713545,
    0.01978196913,
)
INV_SQRT_2PI = 0.3989422804014327


def gelu_pair(x):
    t = 1.0 / (1.0 + 0.25 * jnp.abs(x))
    poly = jnp.full_like(t, TAIL_POLY[-1])
    for coef in TAIL_POLY[-2::-1]:
        poly = poly * t + coef
    bell = jnp.exp2(x * x * (-0.5 * LOG2E))
    below = bell * (t * poly)
    cdf = jnp.where(x >= 0, 1.0 - below, below)
    return x * cdf, cdf + x * (bell * INV_SQRT_2PI)


def dot(a, b):
    return jnp.dot(a, b, preferred_element_type=jnp.float32)


def dot_nt(a, b):
    return lax.dot_general(a, b, (((1,), (1,)), ((), ())), preferred_element_type=jnp.float32)


def dot_tn(a, b):
    return lax.dot_general(a, b, (((0,), (0,)), ((), ())), preferred_element_type=jnp.float32)


def score_bias(seg_row):
    across = jnp.broadcast_to(seg_row, (SEQ_LEN, SEQ_LEN))
    tall = jnp.broadcast_to(seg_row, (PAIR, SEQ_LEN)).T
    along = jnp.concatenate([tall] * (SEQ_LEN // PAIR), axis=1)
    row = lax.broadcasted_iota(jnp.int32, (SEQ_LEN, SEQ_LEN), 0)
    col = lax.broadcasted_iota(jnp.int32, (SEQ_LEN, SEQ_LEN), 1)
    allowed = ((across == along) & (across >= 0)) | (row == col)
    return jnp.where(allowed, 0.0, -1e30)


def head_lanes():
    lane = lax.broadcasted_iota(jnp.int32, (1, PAIR), 1)
    first = (lane < HEAD_DIM).astype(jnp.float32)
    return lane < HEAD_DIM, (first.astype(jnp.bfloat16), (1.0 - first).astype(jnp.bfloat16))


def cols(start, width):
    return pl.ds(pl.multiple_of(start, 128), width)


def attend_kernel(width, hid_ref, seg_ref, w_ref, qkv_ref, ctx_ref, bias_ref):
    step = 256

    def project(c, _):
        at = cols(c * step, step)
        qkv_ref[:, at] = dot(hid_ref[...], w_ref[:, at]).astype(jnp.bfloat16)
        return 0

    lax.fori_loop(0, 3 * width // step, project, 0)
    bias_ref[...] = score_bias(seg_ref[0])
    low, masks = head_lanes()

    def pair(h, _):
        q = qkv_ref[:, cols(h * PAIR, PAIR)]
        k = qkv_ref[:, cols(width + h * PAIR, PAIR)]
        v = qkv_ref[:, cols(2 * width + h * PAIR, PAIR)]
        v_ones = jnp.concatenate([v, jnp.ones_like(v)], axis=1)
        parts = []
        for mask in masks:
            s = dot_nt(q * mask, k) * (SCORE_SCALE * LOG2E) + bias_ref[...]
            e = jnp.exp2(s - jnp.max(s, axis=1, keepdims=True)).astype(jnp.bfloat16)
            o = dot(e, v_ones)
            parts.append(o[:, :PAIR] / o[:, PAIR:])
        ctx_ref[:, cols(h * PAIR, PAIR)] = jnp.where(low, parts[0], parts[1]).astype(jnp.bfloat16)
        return 0

    lax.fori_loop(0, width // PAIR, pair, 0)


def attend_forward(hidden, seg_rows, weight_in):
    rows, width = hidden.shape
    seqs = rows // SEQ_LEN
    return pl.pallas_call(
        lambda *refs: attend_kernel(width, *refs),
        grid=(seqs,),
        out_shape=[
            jax.ShapeDtypeStruct((rows, 3 * width), jnp.bfloat16),
            jax.ShapeDtypeStruct((rows, width), jnp.bfloat16),
        ],
        in_specs=[
            pl.BlockSpec((SEQ_LEN, width), lambda i: (i, 0)),
            pl.BlockSpec((1, 1, SEQ_LEN), lambda i: (i, 0, 0)),
            pl.BlockSpec((width, 3 * width), lambda i: (0, 0)),
        ],
        out_specs=[
            pl.BlockSpec((SEQ_LEN, 3 * width), lambda i: (i, 0)),
            pl.BlockSpec((SEQ_LEN, width), lambda i: (i, 0)),
        ],
        scratch_shapes=[pltpu.VMEM((SEQ_LEN, SEQ_LEN), jnp.float32)],
        compiler_params=pltpu.CompilerParams(vmem_limit_bytes=VMEM_LIMIT),
        cost_estimate=pl.CostEstimate(
            flops=rows * width * (6 * width + 4 * SEQ_LEN),
            bytes_accessed=2 * rows * 5 * width + 6 * width * width,
            transcendentals=rows * SEQ_LEN * width // HEAD_DIM,
        ),
        name="attend_forward",
    )(hidden, seg_rows, weight_in)


def reduce_phases(depth, sums_ref, out_ref, first, second, third, fourth, acc, total, send_sem, recv_sem):
    me = lax.axis_index("dp")
    core = lax.axis_index("head")
    z = me // PLANE
    step_a, step_b = 1 + core, 2 - core
    a, b = (me // step_a) % 2, (me // step_b) % 2
    peer_a = {"dp": z * PLANE + (1 - a) * step_a + b * step_b}
    peer_b = {"dp": z * PLANE + a * step_a + (1 - b) * step_b}
    partner = {"head": 1 - core}
    ring = [{"dp": (z + d) % depth * PLANE + me % PLANE} for d in range(1, depth)]
    half = sums_ref.shape[0] // 2
    quarter, eighth = half // 2, half // 4
    piece = eighth // depth

    def rows(start, size):
        return pl.ds(pl.multiple_of(start, 8), size)

    def send(slot, src, dst, target):
        copy = pltpu.make_async_remote_copy(
            src_ref=src,
            dst_ref=dst,
            send_sem=send_sem.at[slot],
            recv_sem=recv_sem.at[slot],
            device_id=target,
            device_id_type=MESH,
        )
        copy.start()

    def wait(sem, view):
        pltpu.make_async_copy(view, view, sem).wait()

    def arrive(slot, view):
        wait(recv_sem.at[slot], view)
        return view

    base_a = core * half + a * quarter
    base_b = base_a + b * eighth
    local_b = a * quarter + b * eighth
    one, two, three, back_b, back_a, back = range(6)
    out_z = [6 + d for d in range(depth - 1)]
    back_z = [5 + depth + d for d in range(depth - 1)]

    def start():
        barrier = pltpu.get_barrier_semaphore()
        for target in [partner, peer_a, peer_b] + ring:
            pl.semaphore_signal(barrier, inc=1, device_id=target, device_id_type=MESH)
        pl.semaphore_wait(barrier, 2 + depth)
        send(one, sums_ref.at[rows((1 - core) * half, half), :], first, partner)

    def reduce_a():
        arrive(one, first)
        acc[...] = sums_ref[rows(core * half, half), :] + first[...]
        send(two, acc.at[rows((1 - a) * quarter, quarter), :], second, peer_a)

    def reduce_b():
        arrive(two, second)
        acc[rows(a * quarter, quarter), :] += second[...]
        send(three, acc.at[rows(a * quarter + (1 - b) * eighth, eighth), :], third, peer_b)

    def reduce_z():
        arrive(three, third)
        acc[rows(local_b, eighth), :] += third[...]
        for d in range(depth - 1):
            owner = (z + 1 + d) % depth
            src = acc.at[rows(local_b + owner * piece, piece), :]
            send(out_z[d], src, fourth.at[d], ring[d])

    def finish():
        mine = acc[rows(local_b + z * piece, piece), :]
        for d in range(depth - 1):
            arrive(out_z[d], fourth.at[d])
            mine += fourth[d]
        view = total.at[rows(base_b + z * piece, piece), :]
        view[...] = mine
        for d in range(depth - 1):
            send(back_z[d], view, view, ring[d])

    def return_b():
        for d in range(depth - 1):
            sender = (z + depth - 1 - d) % depth
            arrive(back_z[d], total.at[rows(base_b + sender * piece, piece), :])
        view = total.at[rows(base_b, eighth), :]
        send(back_b, view, view, peer_b)

    def return_a():
        arrive(back_b, total.at[rows(base_a + (1 - b) * eighth, eighth), :])
        view = total.at[rows(base_a, quarter), :]
        send(back_a, view, view, peer_a)

    def return_core():
        arrive(back_a, total.at[rows(core * half + (1 - a) * quarter, quarter), :])
        view = total.at[rows(core * half, half), :]
        send(back, view, view, partner)

    def end():
        arrive(back, total.at[rows((1 - core) * half, half), :])
        out_ref[...] = total[...]
        for slot, view in [
            (one, first),
            (two, second),
            (three, third),
            (back_b, third),
            (back_a, second),
            (back, first),
        ]:
            wait(send_sem.at[slot], view)
        for slot in out_z + back_z:
            wait(send_sem.at[slot], fourth.at[0])

    return [start, reduce_a, reduce_b, reduce_z, finish, return_b, return_a, return_core, end]


def attend_grad_kernel(width, depth, *refs):
    qkv_ref, cg_ref, seg_ref, sog_ref, w_ref = refs[:5]
    if depth:
        sums_ref, out_ref, reduced_ref, grad_ref, bias_ref = refs[5:10]
        *phases, end = reduce_phases(depth, sums_ref, reduced_ref, *refs[10:])
    else:
        out_ref, grad_ref, bias_ref = refs[5:]
        phases = []
    turn = pl.program_id(0)
    pairs = width // PAIR
    bias_ref[...] = score_bias(seg_ref[0])
    low, masks = head_lanes()

    def pair(h, _):
        for n, phase in enumerate(phases):
            pl.when(turn * pairs + h == n)(phase)
        q = qkv_ref[:, cols(h * PAIR, PAIR)]
        k = qkv_ref[:, cols(width + h * PAIR, PAIR)]
        v = qkv_ref[:, cols(2 * width + h * PAIR, PAIR)]
        g = cg_ref[:, cols(h * PAIR, PAIR)]
        parts = []
        for mask in masks:
            s = dot_nt(k * mask, q) * (SCORE_SCALE * LOG2E) + bias_ref[...]
            e = jnp.exp2(s - jnp.max(s, axis=0, keepdims=True))
            p = e * (1.0 / jnp.sum(e, axis=0, keepdims=True))
            pg = dot_nt(v * mask, g)
            ds = (p * (pg - jnp.sum(p * pg, axis=0, keepdims=True))).astype(jnp.bfloat16)
            parts.append((dot_tn(ds, k), dot(ds, q), dot(p.astype(jnp.bfloat16), g)))
        for n, scale in enumerate((SCORE_SCALE, SCORE_SCALE, 1.0)):
            both = jnp.where(low, parts[0][n], parts[1][n]) * scale
            grad_ref[:, cols(n * width + h * PAIR, PAIR)] = both.astype(jnp.bfloat16)
        return 0

    lax.fori_loop(0, pairs, pair, 0)
    step = 256

    def back(c, _):
        at = cols(c * step, step)
        out_ref[:, at] = sog_ref[:, at] + dot_nt(grad_ref[...], w_ref[at, :])
        return 0

    lax.fori_loop(0, width // step, back, 0)
    if phases:
        pl.when(turn == pl.num_programs(0) - 1)(end)


def attend_backward(qkv, ctx_grad, seg_rows, sum_one_grad, weight_in, sums):
    rows, width = ctx_grad.shape
    count, span = sums.shape
    size = lax.axis_size("dp")
    depth = size // PLANE
    fits = size % PLANE == 0 and count % (64 * depth) == 0 and rows // SEQ_LEN * (width // PAIR) >= 8
    fits = fits and depth > 1
    if not fits:
        depth = 0
    operands = [qkv, ctx_grad, seg_rows, sum_one_grad, weight_in]
    in_specs = [
        pl.BlockSpec((SEQ_LEN, 3 * width), lambda i: (i, 0)),
        pl.BlockSpec((SEQ_LEN, width), lambda i: (i, 0)),
        pl.BlockSpec((1, 1, SEQ_LEN), lambda i: (i, 0, 0)),
        pl.BlockSpec((SEQ_LEN, width), lambda i: (i, 0)),
        pl.BlockSpec((width, 3 * width), lambda i: (0, 0)),
    ]
    out_shape = [jax.ShapeDtypeStruct((rows, width), jnp.float32)]
    out_specs = [pl.BlockSpec((SEQ_LEN, width), lambda i: (i, 0))]
    scratch = [
        pltpu.VMEM((SEQ_LEN, 3 * width), jnp.bfloat16),
        pltpu.VMEM((SEQ_LEN, SEQ_LEN), jnp.float32),
    ]
    settings = {"vmem_limit_bytes": VMEM_LIMIT}
    if fits:
        operands.append(sums)
        in_specs.append(pl.BlockSpec((count, span), lambda i: (0, 0)))
        out_shape.append(jax.ShapeDtypeStruct((count, span), jnp.float32))
        out_specs.append(pl.BlockSpec((count, span), lambda i: (0, 0)))
        scratch += [
            pltpu.VMEM((count // 2, span), jnp.float32),
            pltpu.VMEM((count // 4, span), jnp.float32),
            pltpu.VMEM((count // 8, span), jnp.float32),
            pltpu.VMEM((depth - 1, count // 8 // depth, span), jnp.float32),
            pltpu.VMEM((count // 2, span), jnp.float32),
            pltpu.VMEM((count, span), jnp.float32),
            pltpu.SemaphoreType.DMA((4 + 2 * depth,)),
            pltpu.SemaphoreType.DMA((4 + 2 * depth,)),
        ]
        settings |= {"collective_id": 1, "has_side_effects": True}
    input_grad, *reduced = pl.pallas_call(
        lambda *refs: attend_grad_kernel(width, depth, *refs),
        grid=(rows // SEQ_LEN,),
        out_shape=out_shape,
        in_specs=in_specs,
        out_specs=out_specs,
        scratch_shapes=scratch,
        compiler_params=pltpu.CompilerParams(**settings),
        cost_estimate=pl.CostEstimate(
            flops=rows * width * (6 * width + 10 * SEQ_LEN),
            bytes_accessed=2 * rows * 8 * width + 6 * width * width,
            transcendentals=rows * SEQ_LEN * width // HEAD_DIM,
        ),
        name="attend_backward",
    )(*operands)
    return input_grad, reduced[0] if fits else lax.psum(sums, ("dp", "head"))


def unpack_kernel(sums_ref, ratio_ref, down_ref, down_bias_ref, up_ref, up_bias_ref, gain_ref, shift_ref):
    rank, width = up_ref.shape[1:]
    tall = sums_ref[: 2 * rank, :width].T
    for k in range(2):
        down_ref[k] = tall[:, k * rank : (k + 1) * rank]
        up_ref[k] = sums_ref[(2 + k) * rank : (3 + k) * rank, :width]
    for n in range(width // 128):
        at = slice(128 * n, 128 * n + 128)
        tile = sums_ref[8 * n : 8 * n + 8, width:]
        up_bias_ref[:, at] = tile[0:2]
        gain_ref[:, at] = tile[2:4]
        shift_ref[:, at] = tile[4:6]
        if n == 0:
            down_bias_ref[...] = tile[6:8, :rank]
        if n == 1:
            ratio_ref[...] = tile[6:7, 0:2] / tile[6:7, 2:3]


def unpack(sums, rank):
    width = sums.shape[1] - 128
    shapes = [(1, 2), (2, width, rank), (2, rank), (2, rank, width)] + [(2, width)] * 3
    ratio, *rest = pl.pallas_call(
        unpack_kernel,
        out_shape=[jax.ShapeDtypeStruct(shape, jnp.float32) for shape in shapes],
        name="unpack",
    )(sums)
    return (ratio.reshape(2), *rest)


def row_mean(x):
    return jnp.mean(x, axis=-1, keepdims=True)


def col_sum(x):
    return jnp.sum(x, axis=0, keepdims=True)


def layer_norm(u, gain, shift):
    centred = u - row_mean(u)
    scale = lax.rsqrt(row_mean(centred * centred) + EPS_NORM)
    hat = centred * scale
    return hat, scale, hat * gain + shift


def layer_norm_grad(hat, scale, gain, grad):
    gg = grad * gain
    return scale * (gg - row_mean(gg) - hat * row_mean(gg * hat))


def middle_kernel(
    ff,
    chunk,
    ctx_ref,
    hid_ref,
    og_ref,
    seg_ref,
    wo_ref,
    we_ref,
    wr_ref,
    down_ref,
    down_bias_ref,
    up_ref,
    up_bias_ref,
    gain_ref,
    shift_ref,
    out_ref,
    sog_ref,
    cg_ref,
    sums_ref,
    small_ref,
    slope_ref,
    normed_ref,
    acc_ref,
):
    rank = up_ref.shape[1]
    width = up_ref.shape[2]

    @pl.when(pl.program_id(0) == 0)
    def _():
        sums_ref[...] = jnp.zeros_like(sums_ref)
        small_ref[...] = jnp.zeros_like(small_ref)

    def adapter(k, a):
        a_low = a.astype(jnp.bfloat16)
        act, slope = gelu_pair(dot(a_low, down_ref[k]) + down_bias_ref[k : k + 1, :])
        act = act.astype(jnp.bfloat16)
        branch = dot(act, up_ref[k]) + up_bias_ref[k : k + 1, :]
        ratio = jnp.sqrt(row_mean(branch * branch)) / jnp.sqrt(row_mean(a * a) + EPS_RATIO)
        return branch, ratio, (a_low, act, slope)

    def add(row, value, start=0):
        small_ref[row : row + 1, start : start + value.shape[1]] += value

    def adapter_grad(k, kept, grad):
        a_low, act, slope = kept
        grad_low = grad.astype(jnp.bfloat16)
        hidden_grad = slope * dot_nt(grad_low, up_ref[k])
        hidden_grad = hidden_grad.astype(jnp.bfloat16)
        sums_ref[k * rank : (k + 1) * rank, :width] += dot_tn(hidden_grad, a_low)
        sums_ref[(2 + k) * rank : (3 + k) * rank, :width] += dot_tn(act, grad_low)
        add(k, col_sum(grad_low.astype(jnp.float32)))
        add(6 + k, col_sum(hidden_grad.astype(jnp.float32)))
        return (grad + dot_nt(hidden_grad, down_ref[k])).astype(jnp.bfloat16)

    gain_one, gain_two = gain_ref[0:1, :], gain_ref[1:2, :]
    attended = dot(ctx_ref[...], wo_ref[...])
    branch, ratio_one, kept_one = adapter(0, attended)
    hat_one, scale_one, normed = layer_norm(
        hid_ref[...].astype(jnp.float32) + attended + branch, gain_one, shift_ref[0:1, :]
    )
    normed_ref[...] = normed.astype(jnp.bfloat16)
    acc_ref[...] = jnp.zeros_like(acc_ref)

    def feed(c, _):
        at = cols(c * chunk, chunk)
        act, slope = gelu_pair(dot(normed_ref[...], we_ref[:, at]))
        slope_ref[:, at] = slope
        acc_ref[...] += dot(act.astype(jnp.bfloat16), wr_ref[at, :])
        return 0

    lax.fori_loop(0, ff // chunk, feed, 0, unroll=2)
    feed_out = acc_ref[...]
    branch, ratio_two, kept_two = adapter(1, feed_out)
    hat_two, scale_two, final = layer_norm(normed + feed_out + branch, gain_two, shift_ref[1:2, :])
    out_ref[...] = final.astype(jnp.bfloat16)

    lane = lax.broadcasted_iota(jnp.int32, (1, 128), 1)
    ratios = jnp.where(lane == 0, ratio_one, jnp.where(lane == 1, ratio_two, 1.0))
    valid = (seg_ref[0] >= 0).astype(jnp.float32)
    stats = jnp.dot(
        jnp.broadcast_to(valid, (8, valid.shape[1])),
        ratios,
        precision=lax.Precision.HIGHEST,
        preferred_element_type=jnp.float32,
    )
    add(6, stats[0:1, :], 128)

    grad = og_ref[...].astype(jnp.float32)
    add(3, col_sum(grad * hat_two))
    add(5, col_sum(grad))
    sum_two_grad = layer_norm_grad(hat_two, scale_two, gain_two, grad)
    normed_ref[...] = adapter_grad(1, kept_two, sum_two_grad)
    acc_ref[...] = sum_two_grad

    def feed_grad(c, _):
        at = cols(c * chunk, chunk)
        inner_grad = slope_ref[:, at] * dot_nt(normed_ref[...], wr_ref[at, :])
        acc_ref[...] += dot_nt(inner_grad.astype(jnp.bfloat16), we_ref[:, at])
        return 0

    lax.fori_loop(0, ff // chunk, feed_grad, 0, unroll=2)
    grad = acc_ref[...]
    add(2, col_sum(grad * hat_one))
    add(4, col_sum(grad))
    sum_one_grad = layer_norm_grad(hat_one, scale_one, gain_one, grad)
    sog_ref[...] = sum_one_grad
    attended_grad = adapter_grad(0, kept_one, sum_one_grad)
    cg_ref[...] = dot_nt(attended_grad, wo_ref[...]).astype(jnp.bfloat16)

    @pl.when(pl.program_id(0) == pl.num_programs(0) - 1)
    def _():
        for n in range(width // 128):
            sums_ref[8 * n : 8 * n + 8, width:] = small_ref[:, 128 * n : 128 * n + 128]


TILE = 256
CHUNK = 512
SUM_ROWS = 256


def middle(ctx, hidden, output_grad, seg_ids, frozen, params):
    rows, width = hidden.shape
    weight_out, weight_expand, weight_reduce = frozen
    ff = weight_expand.shape[1]
    seg_tiles = seg_ids.reshape(rows // TILE, 1, TILE)
    whole = [weight_out, weight_expand, weight_reduce, *params]

    def tile_spec(n):
        return pl.BlockSpec((TILE, n), lambda i: (i, 0))

    def whole_spec(x):
        return pl.BlockSpec(x.shape, lambda i: (0,) * x.ndim, pipeline_mode=pl.Buffered(1))

    return pl.pallas_call(
        lambda *refs: middle_kernel(ff, CHUNK, *refs),
        grid=(rows // TILE,),
        out_shape=[
            jax.ShapeDtypeStruct((rows, width), jnp.bfloat16),
            jax.ShapeDtypeStruct((rows, width), jnp.float32),
            jax.ShapeDtypeStruct((rows, width), jnp.bfloat16),
            jax.ShapeDtypeStruct((SUM_ROWS, width + 128), jnp.float32),
        ],
        in_specs=[tile_spec(width)] * 3
        + [pl.BlockSpec((1, 1, TILE), lambda i: (i, 0, 0))]
        + [whole_spec(x) for x in whole],
        out_specs=[tile_spec(width)] * 3 + [pl.BlockSpec((SUM_ROWS, width + 128), lambda i: (0, 0))],
        scratch_shapes=[
            pltpu.VMEM((8, width), jnp.float32),
            pltpu.VMEM((TILE, ff), jnp.float32),
            pltpu.VMEM((TILE, width), jnp.bfloat16),
            pltpu.VMEM((TILE, width), jnp.float32),
        ],
        compiler_params=pltpu.CompilerParams(vmem_limit_bytes=VMEM_LIMIT),
        cost_estimate=pl.CostEstimate(
            flops=4 * rows * width * (width + 2 * ff),
            bytes_accessed=14 * rows * width + 2 * width * (width + 2 * ff),
            transcendentals=2 * rows * ff,
        ),
        name="middle",
    )(ctx, hidden, output_grad, seg_tiles, *whole)


def body(
    hidden_states,
    segment_ids,
    input_weight,
    output_weight,
    expand_weight,
    reduce_weight,
    adapter_down,
    adapter_down_bias,
    adapter_up,
    adapter_up_bias,
    norm_gain,
    norm_shift,
    output_grad,
):
    weight_in, *frozen = gather_weights(
        [input_weight, output_weight, expand_weight, reduce_weight]
    )
    seg_rows = segment_ids.reshape(-1, 1, SEQ_LEN)
    qkv, ctx = attend_forward(hidden_states, seg_rows, weight_in)
    params = (
        adapter_down,
        adapter_down_bias,
        adapter_up,
        adapter_up_bias,
        norm_gain,
        norm_shift,
    )
    output, sum_one_grad, ctx_grad, sums = middle(
        ctx, hidden_states, output_grad, segment_ids, frozen, params
    )
    input_grad, sums = attend_backward(qkv, ctx_grad, seg_rows, sum_one_grad, weight_in, sums)
    return (output, input_grad, *unpack(sums, adapter_up.shape[1]))


def solution(mesh):
    tokens = P(("dp", "head"), None)
    in_specs = (tokens, P(("dp", "head"))) + (P("dp", None),) * 4 + (P(),) * 6 + (tokens,)
    out_specs = (tokens, tokens) + (P(),) * 7
    return jax.shard_map(body, mesh=mesh, in_specs=in_specs, out_specs=out_specs, check_vma=False)
```

```python
import jax
import jax.numpy as jnp
from jax import lax
from jax.experimental import pallas as pl
from jax.experimental.pallas import tpu as pltpu
from jax.sharding import PartitionSpec as P

MESH = pl.DeviceIdType.MESH
PLANE = 4


def gather_stages(depth, z_first, shards, outs, own_sem, send_sem, recv_sem, pair_send, pair_recv):
    me = lax.axis_index("dp")
    core = lax.axis_index("head")
    z = me // PLANE
    step_a = 1 + core
    step_b = 2 - core
    a = (me // step_a) % 2
    b = (me // step_b) % 2
    peer_a = z * PLANE + (1 - a) * step_a + b * step_b
    peer_b = z * PLANE + a * step_a + (1 - b) * step_b
    up, down = me + PLANE, me - PLANE
    partner = 1 - core

    def has_up():
        return z < depth - 1

    def has_down():
        return z > 0

    count = len(outs)
    pending = []

    def owner(z_of, a_of, b_of):
        return z_of * PLANE + a_of * step_a + b_of * step_b

    def guarded(cond, act):
        if cond is None:
            act()
        else:
            pl.when(cond())(act)

    def send(cond, w, piece, src, dst, direction, slot, target):
        def copy():
            return pltpu.make_async_remote_copy(
                src_ref=src,
                dst_ref=dst,
                send_sem=send_sem.at[w, direction, slot],
                recv_sem=recv_sem.at[w, piece],
                device_id={"dp": target},
                device_id_type=MESH,
            )

        guarded(cond, lambda: copy().start())
        pending.append((cond, w, send_sem, (w, direction, slot)))

    def hand(cond, w, piece, view):
        def copy():
            return pltpu.make_async_remote_copy(
                src_ref=view,
                dst_ref=view,
                send_sem=pair_send.at[w, piece],
                recv_sem=pair_recv.at[w, piece],
                device_id={"head": partner},
                device_id_type=MESH,
            )

        guarded(cond, lambda: copy().start())

    def view_of(w, piece, side):
        half = outs[w].shape[2] // 2
        return outs[w].at[piece, :, pl.ds(pl.multiple_of(side * half, 128), half)]

    def wait(sem, view):
        pltpu.make_async_copy(view, view, sem).wait()

    def arrive(cond, w, piece):
        view = view_of(w, piece, core)
        guarded(cond, lambda: wait(recv_sem.at[w, piece], view))
        return view

    def start():
        barrier = pltpu.get_barrier_semaphore()

        def greet(cond, target):
            guarded(
                cond,
                lambda: pl.semaphore_signal(
                    barrier, inc=1, device_id=target, device_id_type=MESH
                ),
            )

        greet(None, {"dp": peer_a})
        greet(None, {"dp": peer_b})
        greet(None, {"head": partner})
        greet(has_up, {"dp": up})
        greet(has_down, {"dp": down})
        pl.semaphore_wait(barrier, 3 + has_up().astype(jnp.int32) + has_down().astype(jnp.int32))
        for w in range(count):
            half = outs[w].shape[2] // 2
            src = shards[w].at[:, pl.ds(pl.multiple_of(core * half, 128), half)]
            view = view_of(w, me, core)
            send(None, w, me, src, view, 0, 0, peer_a)
            send(has_up, w, me, src, view, 1, 0, up)
            send(has_down, w, me, src, view, 2, 0, down)
            send(None, w, me, src, view, 3, 0, peer_b)
        for w in range(count):
            pltpu.make_async_copy(shards[w], outs[w].at[me], own_sem.at[w]).start()

    def first(w):
        if z_first[w]:
            return
        view = arrive(None, w, peer_a)
        send(has_up, w, peer_a, view, view, 1, 1, up)
        send(has_down, w, peer_a, view, view, 2, 1, down)
        send(None, w, peer_a, view, view, 3, 1, peer_b)
        hand(None, w, peer_a, view)

    def line(w, dist):
        for k, a_of in enumerate((a,) if z_first[w] else (a, 1 - a)):
            slot = 2 * dist + k
            for above in (False, True):
                z_of = z + dist if above else z - dist

                def there(above=above):
                    return z + dist < depth if above else z >= dist

                def onward(above=above):
                    inner = z > 0 if above else z < depth - 1
                    return jnp.logical_and(there(above), inner)

                piece = owner(z_of, a_of, b)
                view = arrive(there, w, piece)
                if above:
                    send(onward, w, piece, view, view, 2, slot, down)
                else:
                    send(onward, w, piece, view, view, 1, slot, up)
                late = 2 * depth * above + slot
                if z_first[w]:
                    send(there, w, piece, view, view, 0, late, peer_a)
                send(there, w, piece, view, view, 3, late, peer_b)
                hand(there, w, piece, view)

    def across(w):
        for z_of in range(depth):
            piece = owner(z_of, 1 - a, b)
            view = arrive(None, w, piece)
            send(None, w, piece, view, view, 3, 4 * depth + z_of, peer_b)
            hand(None, w, piece, view)

    def last(w):
        for z_of in range(depth):
            for a_of in range(2):
                piece = owner(z_of, a_of, 1 - b)
                hand(None, w, piece, arrive(None, w, piece))

    def finish():
        for w in range(count):
            wait(own_sem.at[w], outs[w].at[me])
            for z_of in range(depth):
                for a_of in range(2):
                    for b_of in range(2):
                        piece = owner(z_of, a_of, b_of)

                        def pair(w=w, piece=piece):
                            wait(pair_recv.at[w, piece], view_of(w, piece, partner))
                            wait(pair_send.at[w, piece], view_of(w, piece, core))

                        pl.when(piece != me)(pair)
        for cond, w, sem, at in pending:
            guarded(cond, lambda: wait(sem.at[at], view_of(w, me, core)))

    def firsts():
        for w in range(count):
            first(w)

    stages = [start, firsts]
    for dist in range(1, depth):
        for w in range(count):
            stages.append(lambda w=w, dist=dist: line(w, dist))
    for w in range(count):
        if z_first[w]:
            stages.append(lambda w=w: across(w))
    for w in range(count):
        stages.append(lambda w=w: last(w))
    return stages + [finish]


def gather_scratch(count, size):
    return [
        pltpu.SemaphoreType.DMA((count,)),
        pltpu.SemaphoreType.DMA((count, 4, 5 * (size // PLANE))),
        pltpu.SemaphoreType.DMA((count, size)),
        pltpu.SemaphoreType.DMA((count, size)),
        pltpu.SemaphoreType.DMA((count, size)),
    ]


def gather_fits(weights):
    size = lax.axis_size("dp")
    return (
        size % PLANE == 0
        and size > PLANE
        and all(w.shape[0] % 16 == 0 and w.shape[1] % 256 == 0 for w in weights)
    )


def gather_shapes(weights):
    size = lax.axis_size("dp")
    return [jax.ShapeDtypeStruct((size,) + w.shape, w.dtype) for w in weights]


def join(pieces):
    return pieces.reshape(-1, pieces.shape[-1])


def gather_kernel(depth, *refs):
    for stage in gather_stages(depth, (False,), refs[:1], refs[1:2], *refs[2:]):
        stage()


def gather_first(weight):
    size = lax.axis_size("dp")
    gathered = pl.pallas_call(
        lambda *refs: gather_kernel(size // PLANE, *refs),
        out_shape=gather_shapes([weight]),
        in_specs=[pl.BlockSpec(memory_space=pltpu.VMEM)],
        out_specs=[pl.BlockSpec(memory_space=pl.ANY)],
        scratch_shapes=gather_scratch(1, size),
        compiler_params=pltpu.CompilerParams(collective_id=0, has_side_effects=True),
        name="gather_first",
    )(weight)
    return join(gathered[0])


HEAD_DIM = 64
SEQ_LEN = 512
PAIR = 2 * HEAD_DIM
LOG2E = 1.4426950408889634
EPS_NORM = 1e-12
EPS_RATIO = 1e-06
SCORE_SCALE = 0.125
VMEM_LIMIT = 60 * 1024 * 1024

TAIL_POLY = (
    0.09973556672,
    0.09973643158,
    0.09346635627,
    0.08160309818,
    0.05897520771,
    0.06369893559,
    -0.03171721207,
    0.0955967654,
    -0.08087713545,
    0.01978196913,
)
INV_SQRT_2PI = 0.3989422804014327


def gelu_pair(x):
    t = 1.0 / (1.0 + 0.25 * jnp.abs(x))
    poly = jnp.full_like(t, TAIL_POLY[-1])
    for coef in TAIL_POLY[-2::-1]:
        poly = poly * t + coef
    bell = jnp.exp2(x * x * (-0.5 * LOG2E))
    below = bell * (t * poly)
    cdf = jnp.where(x >= 0, 1.0 - below, below)
    return x * cdf, cdf + x * (bell * INV_SQRT_2PI)


def dot(a, b):
    return jnp.dot(a, b, preferred_element_type=jnp.float32)


def dot_nt(a, b):
    return lax.dot_general(a, b, (((1,), (1,)), ((), ())), preferred_element_type=jnp.float32)


def dot_tn(a, b):
    return lax.dot_general(a, b, (((0,), (0,)), ((), ())), preferred_element_type=jnp.float32)


def score_bias(seg_row):
    across = jnp.broadcast_to(seg_row, (SEQ_LEN, SEQ_LEN))
    tall = jnp.broadcast_to(seg_row, (PAIR, SEQ_LEN)).T
    along = jnp.concatenate([tall] * (SEQ_LEN // PAIR), axis=1)
    row = lax.broadcasted_iota(jnp.int32, (SEQ_LEN, SEQ_LEN), 0)
    col = lax.broadcasted_iota(jnp.int32, (SEQ_LEN, SEQ_LEN), 1)
    allowed = ((across == along) & (across >= 0)) | (row == col)
    return jnp.where(allowed, 0.0, -1e30)


def head_lanes():
    lane = lax.broadcasted_iota(jnp.int32, (1, PAIR), 1)
    first = (lane < HEAD_DIM).astype(jnp.float32)
    return lane < HEAD_DIM, (first.astype(jnp.bfloat16), (1.0 - first).astype(jnp.bfloat16))


def cols(start, width):
    return pl.ds(pl.multiple_of(start, 128), width)


def attend_kernel(width, depth, *refs):
    hid_ref, seg_ref, w_ref = refs[:3]
    if depth:
        shards, (qkv_ref, ctx_ref), outs, bias_ref = refs[3:6], refs[6:8], refs[8:11], refs[11]
        start, *stages, finish = gather_stages(depth, Z_FIRST, shards, outs, *refs[12:])
        pl.when(pl.program_id(0) == 0)(start)
    else:
        qkv_ref, ctx_ref, bias_ref = refs[3:]
        stages = []
    turn = pl.program_id(0)
    pairs = width // PAIR
    step = 256

    def project(c, _):
        at = cols(c * step, step)
        qkv_ref[:, at] = dot(hid_ref[...], w_ref[:, at]).astype(jnp.bfloat16)
        return 0

    lax.fori_loop(0, 3 * width // step, project, 0)
    bias_ref[...] = score_bias(seg_ref[0])
    low, masks = head_lanes()

    def pair(h, _):
        for n, stage in enumerate(stages[: SLOTS]):
            pl.when(turn * pairs + h == n)(stage)
        q = qkv_ref[:, cols(h * PAIR, PAIR)]
        k = qkv_ref[:, cols(width + h * PAIR, PAIR)]
        v = qkv_ref[:, cols(2 * width + h * PAIR, PAIR)]
        v_ones = jnp.concatenate([v, jnp.ones_like(v)], axis=1)
        parts = []
        for mask in masks:
            s = dot_nt(q * mask, k) * (SCORE_SCALE * LOG2E) + bias_ref[...]
            e = jnp.exp2(s - jnp.max(s, axis=1, keepdims=True)).astype(jnp.bfloat16)
            o = dot(e, v_ones)
            parts.append(o[:, :PAIR] / o[:, PAIR:])
        ctx_ref[:, cols(h * PAIR, PAIR)] = jnp.where(low, parts[0], parts[1]).astype(jnp.bfloat16)
        return 0

    lax.fori_loop(0, pairs, pair, 0)
    if stages:

        @pl.when(turn == pl.num_programs(0) - 1)
        def _():
            for stage in stages[SLOTS:]:
                stage()
            finish()


Z_FIRST = (False, False, True)
SLOTS = 12


def attend_forward(hidden, seg_rows, weight_in, shards):
    rows, width = hidden.shape
    size = lax.axis_size("dp")
    fits = gather_fits(shards) and rows // SEQ_LEN * (width // PAIR) >= SLOTS
    depth = size // PLANE if fits else 0
    operands = [hidden, seg_rows, weight_in]
    in_specs = [
        pl.BlockSpec((SEQ_LEN, width), lambda i: (i, 0)),
        pl.BlockSpec((1, 1, SEQ_LEN), lambda i: (i, 0, 0)),
        pl.BlockSpec((width, 3 * width), lambda i: (0, 0)),
    ]
    out_shape = [
        jax.ShapeDtypeStruct((rows, 3 * width), jnp.bfloat16),
        jax.ShapeDtypeStruct((rows, width), jnp.bfloat16),
    ]
    out_specs = [
        pl.BlockSpec((SEQ_LEN, 3 * width), lambda i: (i, 0)),
        pl.BlockSpec((SEQ_LEN, width), lambda i: (i, 0)),
    ]
    scratch = [pltpu.VMEM((SEQ_LEN, SEQ_LEN), jnp.float32)]
    settings = {"vmem_limit_bytes": VMEM_LIMIT}
    if fits:
        operands += shards
        in_specs += [pl.BlockSpec(w.shape, lambda i: (0, 0)) for w in shards]
        out_shape += gather_shapes(shards)
        out_specs += [pl.BlockSpec(memory_space=pl.ANY)] * len(shards)
        scratch += gather_scratch(len(shards), size)
        settings |= {"collective_id": 2, "has_side_effects": True}
    qkv, ctx, *gathered = pl.pallas_call(
        lambda *refs: attend_kernel(width, depth, *refs),
        grid=(rows // SEQ_LEN,),
        out_shape=out_shape,
        in_specs=in_specs,
        out_specs=out_specs,
        scratch_shapes=scratch,
        compiler_params=pltpu.CompilerParams(**settings),
        cost_estimate=pl.CostEstimate(
            flops=rows * width * (6 * width + 4 * SEQ_LEN),
            bytes_accessed=2 * rows * 5 * width + 6 * width * width,
            transcendentals=rows * SEQ_LEN * width // HEAD_DIM,
        ),
        name="attend_forward",
    )(*operands)
    if not fits:
        return qkv, ctx, [lax.all_gather(w, "dp", axis=0, tiled=True) for w in shards]
    return qkv, ctx, [join(pieces) for pieces in gathered]


def reduce_phases(depth, sums_ref, out_ref, first, second, third, fourth, acc, total, send_sem, recv_sem):
    me = lax.axis_index("dp")
    core = lax.axis_index("head")
    z = me // PLANE
    step_a, step_b = 1 + core, 2 - core
    a, b = (me // step_a) % 2, (me // step_b) % 2
    peer_a = {"dp": z * PLANE + (1 - a) * step_a + b * step_b}
    peer_b = {"dp": z * PLANE + a * step_a + (1 - b) * step_b}
    partner = {"head": 1 - core}
    ring = [{"dp": (z + d) % depth * PLANE + me % PLANE} for d in range(1, depth)]
    half = sums_ref.shape[0] // 2
    quarter, eighth = half // 2, half // 4
    piece = eighth // depth

    def rows(start, size):
        return pl.ds(pl.multiple_of(start, 8), size)

    def send(slot, src, dst, target):
        copy = pltpu.make_async_remote_copy(
            src_ref=src,
            dst_ref=dst,
            send_sem=send_sem.at[slot],
            recv_sem=recv_sem.at[slot],
            device_id=target,
            device_id_type=MESH,
        )
        copy.start()

    def wait(sem, view):
        pltpu.make_async_copy(view, view, sem).wait()

    def arrive(slot, view):
        wait(recv_sem.at[slot], view)
        return view

    base_a = core * half + a * quarter
    base_b = base_a + b * eighth
    local_b = a * quarter + b * eighth
    one, two, three, back_b, back_a, back = range(6)
    out_z = [6 + d for d in range(depth - 1)]
    back_z = [5 + depth + d for d in range(depth - 1)]

    def start():
        barrier = pltpu.get_barrier_semaphore()
        for target in [partner, peer_a, peer_b] + ring:
            pl.semaphore_signal(barrier, inc=1, device_id=target, device_id_type=MESH)
        pl.semaphore_wait(barrier, 2 + depth)
        send(one, sums_ref.at[rows((1 - core) * half, half), :], first, partner)

    def reduce_a():
        arrive(one, first)
        acc[...] = sums_ref[rows(core * half, half), :] + first[...]
        send(two, acc.at[rows((1 - a) * quarter, quarter), :], second, peer_a)

    def reduce_b():
        arrive(two, second)
        acc[rows(a * quarter, quarter), :] += second[...]
        send(three, acc.at[rows(a * quarter + (1 - b) * eighth, eighth), :], third, peer_b)

    def reduce_z():
        arrive(three, third)
        acc[rows(local_b, eighth), :] += third[...]
        for d in range(depth - 1):
            owner = (z + 1 + d) % depth
            src = acc.at[rows(local_b + owner * piece, piece), :]
            send(out_z[d], src, fourth.at[d], ring[d])

    def finish():
        mine = acc[rows(local_b + z * piece, piece), :]
        for d in range(depth - 1):
            arrive(out_z[d], fourth.at[d])
            mine += fourth[d]
        view = total.at[rows(base_b + z * piece, piece), :]
        view[...] = mine
        for d in range(depth - 1):
            send(back_z[d], view, view, ring[d])

    def return_b():
        for d in range(depth - 1):
            sender = (z + depth - 1 - d) % depth
            arrive(back_z[d], total.at[rows(base_b + sender * piece, piece), :])
        view = total.at[rows(base_b, eighth), :]
        send(back_b, view, view, peer_b)

    def return_a():
        arrive(back_b, total.at[rows(base_a + (1 - b) * eighth, eighth), :])
        view = total.at[rows(base_a, quarter), :]
        send(back_a, view, view, peer_a)

    def return_core():
        arrive(back_a, total.at[rows(core * half + (1 - a) * quarter, quarter), :])
        view = total.at[rows(core * half, half), :]
        send(back, view, view, partner)

    def end():
        arrive(back, total.at[rows((1 - core) * half, half), :])
        out_ref[...] = total[...]
        for slot, view in [
            (one, first),
            (two, second),
            (three, third),
            (back_b, third),
            (back_a, second),
            (back, first),
        ]:
            wait(send_sem.at[slot], view)
        for slot in out_z + back_z:
            wait(send_sem.at[slot], fourth.at[0])

    return [start, reduce_a, reduce_b, reduce_z, finish, return_b, return_a, return_core, end]


def attend_grad_kernel(width, depth, *refs):
    qkv_ref, cg_ref, seg_ref, sog_ref, w_ref = refs[:5]
    if depth:
        sums_ref, out_ref, reduced_ref, grad_ref, bias_ref = refs[5:10]
        *phases, end = reduce_phases(depth, sums_ref, reduced_ref, *refs[10:])
    else:
        out_ref, grad_ref, bias_ref = refs[5:]
        phases = []
    turn = pl.program_id(0)
    pairs = width // PAIR
    bias_ref[...] = score_bias(seg_ref[0])
    low, masks = head_lanes()

    def pair(h, _):
        for n, phase in zip(REDUCE_SLOTS, phases):
            pl.when(turn * pairs + h == n)(phase)
        q = qkv_ref[:, cols(h * PAIR, PAIR)]
        k = qkv_ref[:, cols(width + h * PAIR, PAIR)]
        v = qkv_ref[:, cols(2 * width + h * PAIR, PAIR)]
        g = cg_ref[:, cols(h * PAIR, PAIR)]
        parts = []
        for mask in masks:
            s = dot_nt(k * mask, q) * (SCORE_SCALE * LOG2E) + bias_ref[...]
            e = jnp.exp2(s - jnp.max(s, axis=0, keepdims=True))
            p = e * (1.0 / jnp.sum(e, axis=0, keepdims=True))
            pg = dot_nt(v * mask, g)
            ds = (p * (pg - jnp.sum(p * pg, axis=0, keepdims=True))).astype(jnp.bfloat16)
            parts.append((dot_tn(ds, k), dot(ds, q), dot(p.astype(jnp.bfloat16), g)))
        for n, scale in enumerate((SCORE_SCALE, SCORE_SCALE, 1.0)):
            both = jnp.where(low, parts[0][n], parts[1][n]) * scale
            grad_ref[:, cols(n * width + h * PAIR, PAIR)] = both.astype(jnp.bfloat16)
        return 0

    lax.fori_loop(0, pairs, pair, 0)
    step = 256

    def back(c, _):
        at = cols(c * step, step)
        out_ref[:, at] = sog_ref[:, at] + dot_nt(grad_ref[...], w_ref[at, :])
        return 0

    lax.fori_loop(0, width // step, back, 0)
    if phases:
        pl.when(turn == pl.num_programs(0) - 1)(end)


REDUCE_SLOTS = (0, 1, 3, 4, 6, 8, 9, 11)


def attend_backward(qkv, ctx_grad, seg_rows, sum_one_grad, weight_in, sums):
    rows, width = ctx_grad.shape
    count, span = sums.shape
    size = lax.axis_size("dp")
    depth = size // PLANE
    fits = size % PLANE == 0 and count % (64 * depth) == 0 and rows // SEQ_LEN * (width // PAIR) > REDUCE_SLOTS[-1]
    fits = fits and depth > 1
    if not fits:
        depth = 0
    operands = [qkv, ctx_grad, seg_rows, sum_one_grad, weight_in]
    in_specs = [
        pl.BlockSpec((SEQ_LEN, 3 * width), lambda i: (i, 0)),
        pl.BlockSpec((SEQ_LEN, width), lambda i: (i, 0)),
        pl.BlockSpec((1, 1, SEQ_LEN), lambda i: (i, 0, 0)),
        pl.BlockSpec((SEQ_LEN, width), lambda i: (i, 0)),
        pl.BlockSpec((width, 3 * width), lambda i: (0, 0)),
    ]
    out_shape = [jax.ShapeDtypeStruct((rows, width), jnp.float32)]
    out_specs = [pl.BlockSpec((SEQ_LEN, width), lambda i: (i, 0))]
    scratch = [
        pltpu.VMEM((SEQ_LEN, 3 * width), jnp.bfloat16),
        pltpu.VMEM((SEQ_LEN, SEQ_LEN), jnp.float32),
    ]
    settings = {"vmem_limit_bytes": VMEM_LIMIT}
    if fits:
        operands.append(sums)
        in_specs.append(pl.BlockSpec((count, span), lambda i: (0, 0)))
        out_shape.append(jax.ShapeDtypeStruct((count, span), jnp.float32))
        out_specs.append(pl.BlockSpec((count, span), lambda i: (0, 0)))
        scratch += [
            pltpu.VMEM((count // 2, span), jnp.float32),
            pltpu.VMEM((count // 4, span), jnp.float32),
            pltpu.VMEM((count // 8, span), jnp.float32),
            pltpu.VMEM((depth - 1, count // 8 // depth, span), jnp.float32),
            pltpu.VMEM((count // 2, span), jnp.float32),
            pltpu.VMEM((count, span), jnp.float32),
            pltpu.SemaphoreType.DMA((4 + 2 * depth,)),
            pltpu.SemaphoreType.DMA((4 + 2 * depth,)),
        ]
        settings |= {"collective_id": 1, "has_side_effects": True}
    input_grad, *reduced = pl.pallas_call(
        lambda *refs: attend_grad_kernel(width, depth, *refs),
        grid=(rows // SEQ_LEN,),
        out_shape=out_shape,
        in_specs=in_specs,
        out_specs=out_specs,
        scratch_shapes=scratch,
        compiler_params=pltpu.CompilerParams(**settings),
        cost_estimate=pl.CostEstimate(
            flops=rows * width * (6 * width + 10 * SEQ_LEN),
            bytes_accessed=2 * rows * 8 * width + 6 * width * width,
            transcendentals=rows * SEQ_LEN * width // HEAD_DIM,
        ),
        name="attend_backward",
    )(*operands)
    return input_grad, reduced[0] if fits else lax.psum(sums, ("dp", "head"))


def unpack_kernel(sums_ref, ratio_ref, down_ref, down_bias_ref, up_ref, up_bias_ref, gain_ref, shift_ref):
    rank, width = up_ref.shape[1:]
    tall = sums_ref[: 2 * rank, :width].T
    for k in range(2):
        down_ref[k] = tall[:, k * rank : (k + 1) * rank]
        up_ref[k] = sums_ref[(2 + k) * rank : (3 + k) * rank, :width]
    for n in range(width // 128):
        at = slice(128 * n, 128 * n + 128)
        tile = sums_ref[8 * n : 8 * n + 8, width:]
        up_bias_ref[:, at] = tile[0:2]
        gain_ref[:, at] = tile[2:4]
        shift_ref[:, at] = tile[4:6]
        if n == 0:
            down_bias_ref[...] = tile[6:8, :rank]
        if n == 1:
            ratio_ref[...] = tile[6:7, 0:2] / tile[6:7, 2:3]


def unpack(sums, rank):
    width = sums.shape[1] - 128
    shapes = [(1, 2), (2, width, rank), (2, rank), (2, rank, width)] + [(2, width)] * 3
    ratio, *rest = pl.pallas_call(
        unpack_kernel,
        out_shape=[jax.ShapeDtypeStruct(shape, jnp.float32) for shape in shapes],
        name="unpack",
    )(sums)
    return (ratio.reshape(2), *rest)


def row_mean(x):
    return jnp.mean(x, axis=-1, keepdims=True)


def col_sum(x):
    return jnp.sum(x, axis=0, keepdims=True)


def layer_norm(u, gain, shift):
    centred = u - row_mean(u)
    scale = lax.rsqrt(row_mean(centred * centred) + EPS_NORM)
    hat = centred * scale
    return hat, scale, hat * gain + shift


def layer_norm_grad(hat, scale, gain, grad):
    gg = grad * gain
    return scale * (gg - row_mean(gg) - hat * row_mean(gg * hat))


def middle_kernel(
    ff,
    chunk,
    ctx_ref,
    hid_ref,
    og_ref,
    seg_ref,
    wo_ref,
    we_ref,
    wr_ref,
    down_ref,
    down_bias_ref,
    up_ref,
    up_bias_ref,
    gain_ref,
    shift_ref,
    out_ref,
    sog_ref,
    cg_ref,
    sums_ref,
    small_ref,
    slope_ref,
    normed_ref,
    acc_ref,
):
    rank = up_ref.shape[1]
    width = up_ref.shape[2]

    @pl.when(pl.program_id(0) == 0)
    def _():
        sums_ref[...] = jnp.zeros_like(sums_ref)
        small_ref[...] = jnp.zeros_like(small_ref)

    def adapter(k, a):
        a_low = a.astype(jnp.bfloat16)
        act, slope = gelu_pair(dot(a_low, down_ref[k]) + down_bias_ref[k : k + 1, :])
        act = act.astype(jnp.bfloat16)
        branch = dot(act, up_ref[k]) + up_bias_ref[k : k + 1, :]
        ratio = jnp.sqrt(row_mean(branch * branch)) / jnp.sqrt(row_mean(a * a) + EPS_RATIO)
        return branch, ratio, (a_low, act, slope)

    def add(row, value, start=0):
        small_ref[row : row + 1, start : start + value.shape[1]] += value

    def adapter_grad(k, kept, grad):
        a_low, act, slope = kept
        grad_low = grad.astype(jnp.bfloat16)
        hidden_grad = slope * dot_nt(grad_low, up_ref[k])
        hidden_grad = hidden_grad.astype(jnp.bfloat16)
        sums_ref[k * rank : (k + 1) * rank, :width] += dot_tn(hidden_grad, a_low)
        sums_ref[(2 + k) * rank : (3 + k) * rank, :width] += dot_tn(act, grad_low)
        add(k, col_sum(grad_low.astype(jnp.float32)))
        add(6 + k, col_sum(hidden_grad.astype(jnp.float32)))
        return (grad + dot_nt(hidden_grad, down_ref[k])).astype(jnp.bfloat16)

    gain_one, gain_two = gain_ref[0:1, :], gain_ref[1:2, :]
    attended = dot(ctx_ref[...], wo_ref[...])
    branch, ratio_one, kept_one = adapter(0, attended)
    hat_one, scale_one, normed = layer_norm(
        hid_ref[...].astype(jnp.float32) + attended + branch, gain_one, shift_ref[0:1, :]
    )
    normed_ref[...] = normed.astype(jnp.bfloat16)
    acc_ref[...] = jnp.zeros_like(acc_ref)

    def feed(c, _):
        at = cols(c * chunk, chunk)
        act, slope = gelu_pair(dot(normed_ref[...], we_ref[:, at]))
        slope_ref[:, at] = slope
        acc_ref[...] += dot(act.astype(jnp.bfloat16), wr_ref[at, :])
        return 0

    lax.fori_loop(0, ff // chunk, feed, 0, unroll=2)
    feed_out = acc_ref[...]
    branch, ratio_two, kept_two = adapter(1, feed_out)
    hat_two, scale_two, final = layer_norm(normed + feed_out + branch, gain_two, shift_ref[1:2, :])
    out_ref[...] = final.astype(jnp.bfloat16)

    lane = lax.broadcasted_iota(jnp.int32, (1, 128), 1)
    ratios = jnp.where(lane == 0, ratio_one, jnp.where(lane == 1, ratio_two, 1.0))
    valid = (seg_ref[0] >= 0).astype(jnp.float32)
    stats = jnp.dot(
        jnp.broadcast_to(valid, (8, valid.shape[1])),
        ratios,
        precision=lax.Precision.HIGHEST,
        preferred_element_type=jnp.float32,
    )
    add(6, stats[0:1, :], 128)

    grad = og_ref[...].astype(jnp.float32)
    add(3, col_sum(grad * hat_two))
    add(5, col_sum(grad))
    sum_two_grad = layer_norm_grad(hat_two, scale_two, gain_two, grad)
    normed_ref[...] = adapter_grad(1, kept_two, sum_two_grad)
    acc_ref[...] = sum_two_grad

    def feed_grad(c, _):
        at = cols(c * chunk, chunk)
        inner_grad = slope_ref[:, at] * dot_nt(normed_ref[...], wr_ref[at, :])
        acc_ref[...] += dot_nt(inner_grad.astype(jnp.bfloat16), we_ref[:, at])
        return 0

    lax.fori_loop(0, ff // chunk, feed_grad, 0, unroll=2)
    grad = acc_ref[...]
    add(2, col_sum(grad * hat_one))
    add(4, col_sum(grad))
    sum_one_grad = layer_norm_grad(hat_one, scale_one, gain_one, grad)
    sog_ref[...] = sum_one_grad
    attended_grad = adapter_grad(0, kept_one, sum_one_grad)
    cg_ref[...] = dot_nt(attended_grad, wo_ref[...]).astype(jnp.bfloat16)

    @pl.when(pl.program_id(0) == pl.num_programs(0) - 1)
    def _():
        for n in range(width // 128):
            sums_ref[8 * n : 8 * n + 8, width:] = small_ref[:, 128 * n : 128 * n + 128]


TILE = 256
CHUNK = 512
SUM_ROWS = 256


def middle(ctx, hidden, output_grad, seg_ids, frozen, params):
    rows, width = hidden.shape
    weight_out, weight_expand, weight_reduce = frozen
    ff = weight_expand.shape[1]
    seg_tiles = seg_ids.reshape(rows // TILE, 1, TILE)
    whole = [weight_out, weight_expand, weight_reduce, *params]

    def tile_spec(n):
        return pl.BlockSpec((TILE, n), lambda i: (i, 0))

    def whole_spec(x):
        return pl.BlockSpec(x.shape, lambda i: (0,) * x.ndim, pipeline_mode=pl.Buffered(1))

    return pl.pallas_call(
        lambda *refs: middle_kernel(ff, CHUNK, *refs),
        grid=(rows // TILE,),
        out_shape=[
            jax.ShapeDtypeStruct((rows, width), jnp.bfloat16),
            jax.ShapeDtypeStruct((rows, width), jnp.float32),
            jax.ShapeDtypeStruct((rows, width), jnp.bfloat16),
            jax.ShapeDtypeStruct((SUM_ROWS, width + 128), jnp.float32),
        ],
        in_specs=[tile_spec(width)] * 3
        + [pl.BlockSpec((1, 1, TILE), lambda i: (i, 0, 0))]
        + [whole_spec(x) for x in whole],
        out_specs=[tile_spec(width)] * 3 + [pl.BlockSpec((SUM_ROWS, width + 128), lambda i: (0, 0))],
        scratch_shapes=[
            pltpu.VMEM((8, width), jnp.float32),
            pltpu.VMEM((TILE, ff), jnp.float32),
            pltpu.VMEM((TILE, width), jnp.bfloat16),
            pltpu.VMEM((TILE, width), jnp.float32),
        ],
        compiler_params=pltpu.CompilerParams(vmem_limit_bytes=VMEM_LIMIT),
        cost_estimate=pl.CostEstimate(
            flops=4 * rows * width * (width + 2 * ff),
            bytes_accessed=14 * rows * width + 2 * width * (width + 2 * ff),
            transcendentals=2 * rows * ff,
        ),
        name="middle",
    )(ctx, hidden, output_grad, seg_tiles, *whole)


def body(
    hidden_states,
    segment_ids,
    input_weight,
    output_weight,
    expand_weight,
    reduce_weight,
    adapter_down,
    adapter_down_bias,
    adapter_up,
    adapter_up_bias,
    norm_gain,
    norm_shift,
    output_grad,
):
    if gather_fits([input_weight]):
        weight_in = gather_first(input_weight)
    else:
        weight_in = lax.all_gather(input_weight, "dp", axis=0, tiled=True)
    seg_rows = segment_ids.reshape(-1, 1, SEQ_LEN)
    shards = [output_weight, expand_weight, reduce_weight]
    qkv, ctx, frozen = attend_forward(hidden_states, seg_rows, weight_in, shards)
    params = (
        adapter_down,
        adapter_down_bias,
        adapter_up,
        adapter_up_bias,
        norm_gain,
        norm_shift,
    )
    output, sum_one_grad, ctx_grad, sums = middle(
        ctx, hidden_states, output_grad, segment_ids, frozen, params
    )
    input_grad, sums = attend_backward(qkv, ctx_grad, seg_rows, sum_one_grad, weight_in, sums)
    return (output, input_grad, *unpack(sums, adapter_up.shape[1]))


def solution(mesh):
    tokens = P(("dp", "head"), None)
    in_specs = (tokens, P(("dp", "head"))) + (P("dp", None),) * 4 + (P(),) * 6 + (tokens,)
    out_specs = (tokens, tokens) + (P(),) * 7
    return jax.shard_map(body, mesh=mesh, in_specs=in_specs, out_specs=out_specs, check_vma=False)
```

```python
import jax
import jax.numpy as jnp
from jax import lax
from jax.experimental import pallas as pl
from jax.experimental.pallas import tpu as pltpu
from jax.sharding import PartitionSpec as P

MESH = pl.DeviceIdType.MESH
PLANE = 4


def gather_stages(depth, units, shards, outs, own_sem, send_sem, recv_sem, pair_send, pair_recv):
    me = lax.axis_index("dp")
    core = lax.axis_index("head")
    z = me // PLANE
    step_a = 1 + core
    step_b = 2 - core
    a = (me // step_a) % 2
    b = (me // step_b) % 2
    partner = 1 - core
    others = [(z + d) % depth for d in range(1, depth)]
    senders = [(z + depth - d) % depth for d in range(1, depth)]
    to_a, to_b, to_z = 0, depth, 2 * depth

    def owner(z_of, a_of, b_of):
        return z_of * PLANE + a_of * step_a + b_of * step_b

    peer_a = owner(z, 1 - a, b)
    peer_b = owner(z, a, 1 - b)

    def view_of(u, piece, side):
        w, row, height, col, span, _ = units[u]
        half = outs[w].shape[2] // 2
        at = pl.ds(pl.multiple_of(side * half + col, 128), span)
        return outs[w].at[piece, row : row + height, at]

    def shard_of(u):
        w, row, height, col, span, _ = units[u]
        half = outs[w].shape[2] // 2
        at = pl.ds(pl.multiple_of(core * half + col, 128), span)
        return shards[w].at[row : row + height, at]

    def wait(sem, view):
        pltpu.make_async_copy(view, view, sem).wait()

    def send(u, piece, src, slot, target):
        pltpu.make_async_remote_copy(
            src_ref=src,
            dst_ref=view_of(u, piece, core),
            send_sem=send_sem.at[u, slot],
            recv_sem=recv_sem.at[u, piece],
            device_id={"dp": target},
            device_id_type=MESH,
        ).start()

    def hand(u, piece):
        view = view_of(u, piece, core)
        pltpu.make_async_remote_copy(
            src_ref=view,
            dst_ref=view,
            send_sem=pair_send.at[u, piece],
            recv_sem=pair_recv.at[u, piece],
            device_id={"head": partner},
            device_id_type=MESH,
        ).start()

    def arrive(u, piece):
        view = view_of(u, piece, core)
        wait(recv_sem.at[u, piece], view)
        return view

    def z_slot(k, d):
        return to_z + k * (depth - 1) + d

    def b_slot(k):
        return to_z + 2 * (depth - 1) + k

    def start():
        barrier = pltpu.get_barrier_semaphore()
        targets = [{"head": partner}, {"dp": peer_a}, {"dp": peer_b}]
        targets += [{"dp": owner(z_of, a, b)} for z_of in others]
        for target in targets:
            pl.semaphore_signal(barrier, inc=1, device_id=target, device_id_type=MESH)
        pl.semaphore_wait(barrier, depth + 2)
        for u in range(len(units)):
            src = shard_of(u)
            send(u, me, src, to_a, peer_a)
            for d, z_of in enumerate(others):
                send(u, me, src, z_slot(0, d), owner(z_of, a, b))
            send(u, me, src, to_b, peer_b)
        for w in range(len(outs)):
            pltpu.make_async_copy(shards[w], outs[w].at[me], own_sem.at[w]).start()

    def first(u):
        view = arrive(u, peer_a)
        for d, z_of in enumerate(others):
            send(u, peer_a, view, z_slot(1, d), owner(z_of, a, b))
        send(u, peer_a, view, to_b + 1, peer_b)
        hand(u, peer_a)

    def line(u):
        along = units[u][5]
        for d, z_of in enumerate(senders):
            for k, a_of in enumerate((a,) if along else (a, 1 - a)):
                piece = owner(z_of, a_of, b)
                view = arrive(u, piece)
                if along:
                    send(u, piece, view, to_a + 1 + d, peer_a)
                send(u, piece, view, b_slot(2 * d + k), peer_b)
                hand(u, piece)

    def across(u):
        for n, z_of in enumerate([z] + senders):
            piece = owner(z_of, 1 - a, b)
            view = arrive(u, piece)
            send(u, piece, view, b_slot(2 * n - 1) if n else to_b + 1, peer_b)
            hand(u, piece)

    def last(u):
        for z_of in [z] + senders:
            for a_of in (a, 1 - a):
                piece = owner(z_of, a_of, 1 - b)
                arrive(u, piece)
                hand(u, piece)

    def finish():
        for w in range(len(outs)):
            wait(own_sem.at[w], outs[w].at[me])
        for u, unit in enumerate(units):
            for z_of in range(depth):
                for a_of in range(2):
                    for b_of in range(2):
                        piece = owner(z_of, a_of, b_of)

                        def pair(u=u, piece=piece):
                            wait(pair_recv.at[u, piece], view_of(u, piece, partner))
                            wait(pair_send.at[u, piece], view_of(u, piece, core))

                        pl.when(piece != me)(pair)
            slots = [to_a, to_b, to_b + 1]
            slots += [z_slot(k, d) for k in range(1 if unit[5] else 2) for d in range(depth - 1)]
            slots += [b_slot(n) for n in range(2 * (depth - 1))]
            if unit[5]:
                slots += [to_a + 1 + d for d in range(depth - 1)]
            for slot in slots:
                wait(send_sem.at[u, slot], view_of(u, me, core))

    return start, first, line, across, last, finish


def gather_scratch(count, units, size):
    return [
        pltpu.SemaphoreType.DMA((count,)),
        pltpu.SemaphoreType.DMA((units, 6 * (size // PLANE))),
        pltpu.SemaphoreType.DMA((units, size)),
        pltpu.SemaphoreType.DMA((units, size)),
        pltpu.SemaphoreType.DMA((units, size)),
    ]


def gather_fits(weights):
    size = lax.axis_size("dp")
    return (
        size % PLANE == 0
        and size > PLANE
        and all(w.shape[0] % 16 == 0 and w.shape[1] % 768 == 0 for w in weights)
        and weights[-1].shape[0] % 32 in (0, 16 * (len(weights) == 1))
    )


def gather_shapes(weights):
    size = lax.axis_size("dp")
    return [jax.ShapeDtypeStruct((size,) + w.shape, w.dtype) for w in weights]


def join(pieces):
    return pieces.reshape(-1, pieces.shape[-1])


def first_units(weight):
    rows, width = weight.shape
    third = width // 6
    return [(0, 0, rows, n * third, third, n > 0) for n in range(3)]


def gather_kernel(depth, units, *refs):
    start, first, line, across, last, finish = gather_stages(
        depth, units, refs[:1], refs[1:2], *refs[2:]
    )
    start()
    first(0)
    for u in (1, 2, 0):
        line(u)
    for u in (1, 2):
        across(u)
    for u in (0, 1, 2):
        last(u)
    finish()


def gather_first(weight):
    size = lax.axis_size("dp")
    units = first_units(weight)
    gathered = pl.pallas_call(
        lambda *refs: gather_kernel(size // PLANE, units, *refs),
        out_shape=gather_shapes([weight]),
        in_specs=[pl.BlockSpec(memory_space=pltpu.VMEM)],
        out_specs=[pl.BlockSpec(memory_space=pl.ANY)],
        scratch_shapes=gather_scratch(1, len(units), size),
        compiler_params=pltpu.CompilerParams(collective_id=0, has_side_effects=True),
        name="gather_first",
    )(weight)
    return join(gathered[0])


def later_units(weights):
    out, expand, reduce = (w.shape for w in weights)
    quarter = expand[1] // 4
    rows = reduce[0] // 2
    return [
        (0, 0, out[0], 0, out[1] // 2, False),
        (1, 0, expand[0], 0, quarter, False),
        (1, 0, expand[0], quarter, quarter, True),
        (2, 0, rows, 0, reduce[1] // 2, True),
        (2, rows, rows, 0, reduce[1] // 2, True),
    ]


def later_stages(start, first, line, across, last, finish):
    def both(one, two):
        def run():
            one()
            two()

        return run

    def of(act, u):
        return lambda: act(u)

    return [
        both(of(first, 0), of(first, 1)),
        of(line, 2),
        of(line, 3),
        of(line, 4),
        of(line, 0),
        of(across, 2),
        of(line, 1),
        of(across, 3),
        of(across, 4),
        both(of(last, 0), of(last, 2)),
        of(last, 1),
        of(last, 3),
        of(last, 4),
    ]


HEAD_DIM = 64
SEQ_LEN = 512
PAIR = 2 * HEAD_DIM
LOG2E = 1.4426950408889634
EPS_NORM = 1e-12
EPS_RATIO = 1e-06
SCORE_SCALE = 0.125
VMEM_LIMIT = 60 * 1024 * 1024

TAIL_POLY = (
    0.09973556672,
    0.09973643158,
    0.09346635627,
    0.08160309818,
    0.05897520771,
    0.06369893559,
    -0.03171721207,
    0.0955967654,
    -0.08087713545,
    0.01978196913,
)
INV_SQRT_2PI = 0.3989422804014327


def gelu_pair(x):
    t = 1.0 / (1.0 + 0.25 * jnp.abs(x))
    poly = jnp.full_like(t, TAIL_POLY[-1])
    for coef in TAIL_POLY[-2::-1]:
        poly = poly * t + coef
    bell = jnp.exp2(x * x * (-0.5 * LOG2E))
    below = bell * (t * poly)
    cdf = jnp.where(x >= 0, 1.0 - below, below)
    return x * cdf, cdf + x * (bell * INV_SQRT_2PI)


def dot(a, b):
    return jnp.dot(a, b, preferred_element_type=jnp.float32)


def dot_nt(a, b):
    return lax.dot_general(a, b, (((1,), (1,)), ((), ())), preferred_element_type=jnp.float32)


def dot_tn(a, b):
    return lax.dot_general(a, b, (((0,), (0,)), ((), ())), preferred_element_type=jnp.float32)


def score_bias(seg_row):
    across = jnp.broadcast_to(seg_row, (SEQ_LEN, SEQ_LEN))
    tall = jnp.broadcast_to(seg_row, (PAIR, SEQ_LEN)).T
    along = jnp.concatenate([tall] * (SEQ_LEN // PAIR), axis=1)
    row = lax.broadcasted_iota(jnp.int32, (SEQ_LEN, SEQ_LEN), 0)
    col = lax.broadcasted_iota(jnp.int32, (SEQ_LEN, SEQ_LEN), 1)
    allowed = ((across == along) & (across >= 0)) | (row == col)
    return jnp.where(allowed, 0.0, -1e30)


def head_lanes():
    lane = lax.broadcasted_iota(jnp.int32, (1, PAIR), 1)
    first = (lane < HEAD_DIM).astype(jnp.float32)
    return lane < HEAD_DIM, (first.astype(jnp.bfloat16), (1.0 - first).astype(jnp.bfloat16))


def cols(start, width):
    return pl.ds(pl.multiple_of(start, 128), width)


def attend_kernel(width, depth, units, *refs):
    hid_ref, seg_ref, w_ref = refs[:3]
    if depth:
        shards, (qkv_ref, ctx_ref), outs, bias_ref = refs[3:6], refs[6:8], refs[8:11], refs[11]
        moves = gather_stages(depth, units, shards, outs, *refs[12:])
        stages = later_stages(*moves)
        start, finish = moves[0], moves[-1]
        pl.when(pl.program_id(0) == 0)(start)
    else:
        qkv_ref, ctx_ref, bias_ref = refs[3:]
        stages = []
    turn = pl.program_id(0)
    pairs = width // PAIR
    step = 256

    def project(c, _):
        at = cols(c * step, step)
        qkv_ref[:, at] = dot(hid_ref[...], w_ref[:, at]).astype(jnp.bfloat16)
        return 0

    lax.fori_loop(0, 3 * width // step, project, 0)
    bias_ref[...] = score_bias(seg_ref[0])
    low, masks = head_lanes()

    def pair(h, _):
        for n, stage in enumerate(stages[: SLOTS]):
            pl.when(turn * pairs + h == n)(stage)
        q = qkv_ref[:, cols(h * PAIR, PAIR)]
        k = qkv_ref[:, cols(width + h * PAIR, PAIR)]
        v = qkv_ref[:, cols(2 * width + h * PAIR, PAIR)]
        v_ones = jnp.concatenate([v, jnp.ones_like(v)], axis=1)
        parts = []
        for mask in masks:
            s = dot_nt(q * mask, k) * (SCORE_SCALE * LOG2E) + bias_ref[...]
            e = jnp.exp2(s - jnp.max(s, axis=1, keepdims=True)).astype(jnp.bfloat16)
            o = dot(e, v_ones)
            parts.append(o[:, :PAIR] / o[:, PAIR:])
        ctx_ref[:, cols(h * PAIR, PAIR)] = jnp.where(low, parts[0], parts[1]).astype(jnp.bfloat16)
        return 0

    lax.fori_loop(0, pairs, pair, 0)
    if stages:

        @pl.when(turn == pl.num_programs(0) - 1)
        def _():
            for stage in stages[SLOTS:]:
                stage()
            finish()


SLOTS = 12


def attend_forward(hidden, seg_rows, weight_in, shards):
    rows, width = hidden.shape
    size = lax.axis_size("dp")
    fits = gather_fits(shards) and rows // SEQ_LEN * (width // PAIR) >= SLOTS
    depth = size // PLANE if fits else 0
    units = later_units(shards)
    operands = [hidden, seg_rows, weight_in]
    in_specs = [
        pl.BlockSpec((SEQ_LEN, width), lambda i: (i, 0)),
        pl.BlockSpec((1, 1, SEQ_LEN), lambda i: (i, 0, 0)),
        pl.BlockSpec((width, 3 * width), lambda i: (0, 0)),
    ]
    out_shape = [
        jax.ShapeDtypeStruct((rows, 3 * width), jnp.bfloat16),
        jax.ShapeDtypeStruct((rows, width), jnp.bfloat16),
    ]
    out_specs = [
        pl.BlockSpec((SEQ_LEN, 3 * width), lambda i: (i, 0)),
        pl.BlockSpec((SEQ_LEN, width), lambda i: (i, 0)),
    ]
    scratch = [pltpu.VMEM((SEQ_LEN, SEQ_LEN), jnp.float32)]
    settings = {"vmem_limit_bytes": VMEM_LIMIT}
    if fits:
        operands += shards
        in_specs += [pl.BlockSpec(w.shape, lambda i: (0, 0)) for w in shards]
        out_shape += gather_shapes(shards)
        out_specs += [pl.BlockSpec(memory_space=pl.ANY)] * len(shards)
        scratch += gather_scratch(len(shards), len(units), size)
        settings |= {"collective_id": 2, "has_side_effects": True}
    qkv, ctx, *gathered = pl.pallas_call(
        lambda *refs: attend_kernel(width, depth, units, *refs),
        grid=(rows // SEQ_LEN,),
        out_shape=out_shape,
        in_specs=in_specs,
        out_specs=out_specs,
        scratch_shapes=scratch,
        compiler_params=pltpu.CompilerParams(**settings),
        cost_estimate=pl.CostEstimate(
            flops=rows * width * (6 * width + 4 * SEQ_LEN),
            bytes_accessed=2 * rows * 5 * width + 6 * width * width,
            transcendentals=rows * SEQ_LEN * width // HEAD_DIM,
        ),
        name="attend_forward",
    )(*operands)
    if not fits:
        return qkv, ctx, [lax.all_gather(w, "dp", axis=0, tiled=True) for w in shards]
    return qkv, ctx, [join(pieces) for pieces in gathered]


def reduce_phases(depth, sums_ref, out_ref, first, second, third, fourth, acc, total, send_sem, recv_sem):
    me = lax.axis_index("dp")
    core = lax.axis_index("head")
    z = me // PLANE
    step_a, step_b = 1 + core, 2 - core
    a, b = (me // step_a) % 2, (me // step_b) % 2
    peer_a = {"dp": z * PLANE + (1 - a) * step_a + b * step_b}
    peer_b = {"dp": z * PLANE + a * step_a + (1 - b) * step_b}
    partner = {"head": 1 - core}
    ring = [{"dp": (z + d) % depth * PLANE + me % PLANE} for d in range(1, depth)]
    half = sums_ref.shape[0] // 2
    quarter, eighth = half // 2, half // 4
    piece = eighth // depth

    def rows(start, size):
        return pl.ds(pl.multiple_of(start, 8), size)

    def send(slot, src, dst, target):
        copy = pltpu.make_async_remote_copy(
            src_ref=src,
            dst_ref=dst,
            send_sem=send_sem.at[slot],
            recv_sem=recv_sem.at[slot],
            device_id=target,
            device_id_type=MESH,
        )
        copy.start()

    def wait(sem, view):
        pltpu.make_async_copy(view, view, sem).wait()

    def arrive(slot, view):
        wait(recv_sem.at[slot], view)
        return view

    base_a = core * half + a * quarter
    base_b = base_a + b * eighth
    local_b = a * quarter + b * eighth
    one, two, three, back_b, back_a, back = range(6)
    out_z = [6 + d for d in range(depth - 1)]
    back_z = [5 + depth + d for d in range(depth - 1)]

    def start():
        barrier = pltpu.get_barrier_semaphore()
        for target in [partner, peer_a, peer_b] + ring:
            pl.semaphore_signal(barrier, inc=1, device_id=target, device_id_type=MESH)
        pl.semaphore_wait(barrier, 2 + depth)
        send(one, sums_ref.at[rows((1 - core) * half, half), :], first, partner)

    def reduce_a():
        arrive(one, first)
        acc[...] = sums_ref[rows(core * half, half), :] + first[...]
        send(two, acc.at[rows((1 - a) * quarter, quarter), :], second, peer_a)

    def reduce_b():
        arrive(two, second)
        acc[rows(a * quarter, quarter), :] += second[...]
        send(three, acc.at[rows(a * quarter + (1 - b) * eighth, eighth), :], third, peer_b)

    def reduce_z():
        arrive(three, third)
        acc[rows(local_b, eighth), :] += third[...]
        for d in range(depth - 1):
            owner = (z + 1 + d) % depth
            src = acc.at[rows(local_b + owner * piece, piece), :]
            send(out_z[d], src, fourth.at[d], ring[d])

    def finish():
        mine = acc[rows(local_b + z * piece, piece), :]
        for d in range(depth - 1):
            arrive(out_z[d], fourth.at[d])
            mine += fourth[d]
        view = total.at[rows(base_b + z * piece, piece), :]
        view[...] = mine
        for d in range(depth - 1):
            send(back_z[d], view, view, ring[d])

    def return_b():
        for d in range(depth - 1):
            sender = (z + depth - 1 - d) % depth
            arrive(back_z[d], total.at[rows(base_b + sender * piece, piece), :])
        view = total.at[rows(base_b, eighth), :]
        send(back_b, view, view, peer_b)

    def return_a():
        arrive(back_b, total.at[rows(base_a + (1 - b) * eighth, eighth), :])
        view = total.at[rows(base_a, quarter), :]
        send(back_a, view, view, peer_a)

    def return_core():
        arrive(back_a, total.at[rows(core * half + (1 - a) * quarter, quarter), :])
        view = total.at[rows(core * half, half), :]
        send(back, view, view, partner)

    def end():
        arrive(back, total.at[rows((1 - core) * half, half), :])
        out_ref[...] = total[...]
        for slot, view in [
            (one, first),
            (two, second),
            (three, third),
            (back_b, third),
            (back_a, second),
            (back, first),
        ]:
            wait(send_sem.at[slot], view)
        for slot in out_z + back_z:
            wait(send_sem.at[slot], fourth.at[0])

    return [start, reduce_a, reduce_b, reduce_z, finish, return_b, return_a, return_core, end]


def attend_grad_kernel(width, depth, *refs):
    qkv_ref, cg_ref, seg_ref, sog_ref, w_ref = refs[:5]
    if depth:
        sums_ref, out_ref, reduced_ref, grad_ref, bias_ref = refs[5:10]
        *phases, end = reduce_phases(depth, sums_ref, reduced_ref, *refs[10:])
    else:
        out_ref, grad_ref, bias_ref = refs[5:]
        phases = []
    turn = pl.program_id(0)
    pairs = width // PAIR
    bias_ref[...] = score_bias(seg_ref[0])
    low, masks = head_lanes()

    def pair(h, _):
        for n, phase in zip(REDUCE_SLOTS, phases):
            pl.when(turn * pairs + h == n)(phase)
        q = qkv_ref[:, cols(h * PAIR, PAIR)]
        k = qkv_ref[:, cols(width + h * PAIR, PAIR)]
        v = qkv_ref[:, cols(2 * width + h * PAIR, PAIR)]
        g = cg_ref[:, cols(h * PAIR, PAIR)]
        parts = []
        for mask in masks:
            s = dot_nt(k * mask, q) * (SCORE_SCALE * LOG2E) + bias_ref[...]
            e = jnp.exp2(s - jnp.max(s, axis=0, keepdims=True))
            p = e * (1.0 / jnp.sum(e, axis=0, keepdims=True))
            pg = dot_nt(v * mask, g)
            ds = (p * (pg - jnp.sum(p * pg, axis=0, keepdims=True))).astype(jnp.bfloat16)
            parts.append((dot_tn(ds, k), dot(ds, q), dot(p.astype(jnp.bfloat16), g)))
        for n, scale in enumerate((SCORE_SCALE, SCORE_SCALE, 1.0)):
            both = jnp.where(low, parts[0][n], parts[1][n]) * scale
            grad_ref[:, cols(n * width + h * PAIR, PAIR)] = both.astype(jnp.bfloat16)
        return 0

    lax.fori_loop(0, pairs, pair, 0)
    step = 256

    def back(c, _):
        at = cols(c * step, step)
        out_ref[:, at] = sog_ref[:, at] + dot_nt(grad_ref[...], w_ref[at, :])
        return 0

    lax.fori_loop(0, width // step, back, 0)
    if phases:
        pl.when(turn == pl.num_programs(0) - 1)(end)


REDUCE_SLOTS = (0, 1, 3, 4, 6, 8, 9, 11)


def attend_backward(qkv, ctx_grad, seg_rows, sum_one_grad, weight_in, sums):
    rows, width = ctx_grad.shape
    count, span = sums.shape
    size = lax.axis_size("dp")
    depth = size // PLANE
    fits = size % PLANE == 0 and count % (64 * depth) == 0 and rows // SEQ_LEN * (width // PAIR) > REDUCE_SLOTS[-1]
    fits = fits and depth > 1
    if not fits:
        depth = 0
    operands = [qkv, ctx_grad, seg_rows, sum_one_grad, weight_in]
    in_specs = [
        pl.BlockSpec((SEQ_LEN, 3 * width), lambda i: (i, 0)),
        pl.BlockSpec((SEQ_LEN, width), lambda i: (i, 0)),
        pl.BlockSpec((1, 1, SEQ_LEN), lambda i: (i, 0, 0)),
        pl.BlockSpec((SEQ_LEN, width), lambda i: (i, 0)),
        pl.BlockSpec((width, 3 * width), lambda i: (0, 0)),
    ]
    out_shape = [jax.ShapeDtypeStruct((rows, width), jnp.float32)]
    out_specs = [pl.BlockSpec((SEQ_LEN, width), lambda i: (i, 0))]
    scratch = [
        pltpu.VMEM((SEQ_LEN, 3 * width), jnp.bfloat16),
        pltpu.VMEM((SEQ_LEN, SEQ_LEN), jnp.float32),
    ]
    settings = {"vmem_limit_bytes": VMEM_LIMIT}
    if fits:
        operands.append(sums)
        in_specs.append(pl.BlockSpec((count, span), lambda i: (0, 0)))
        out_shape.append(jax.ShapeDtypeStruct((count, span), jnp.float32))
        out_specs.append(pl.BlockSpec((count, span), lambda i: (0, 0)))
        scratch += [
            pltpu.VMEM((count // 2, span), jnp.float32),
            pltpu.VMEM((count // 4, span), jnp.float32),
            pltpu.VMEM((count // 8, span), jnp.float32),
            pltpu.VMEM((depth - 1, count // 8 // depth, span), jnp.float32),
            pltpu.VMEM((count // 2, span), jnp.float32),
            pltpu.VMEM((count, span), jnp.float32),
            pltpu.SemaphoreType.DMA((4 + 2 * depth,)),
            pltpu.SemaphoreType.DMA((4 + 2 * depth,)),
        ]
        settings |= {"collective_id": 1, "has_side_effects": True}
    input_grad, *reduced = pl.pallas_call(
        lambda *refs: attend_grad_kernel(width, depth, *refs),
        grid=(rows // SEQ_LEN,),
        out_shape=out_shape,
        in_specs=in_specs,
        out_specs=out_specs,
        scratch_shapes=scratch,
        compiler_params=pltpu.CompilerParams(**settings),
        cost_estimate=pl.CostEstimate(
            flops=rows * width * (6 * width + 10 * SEQ_LEN),
            bytes_accessed=2 * rows * 8 * width + 6 * width * width,
            transcendentals=rows * SEQ_LEN * width // HEAD_DIM,
        ),
        name="attend_backward",
    )(*operands)
    return input_grad, reduced[0] if fits else lax.psum(sums, ("dp", "head"))


def unpack_kernel(sums_ref, ratio_ref, down_ref, down_bias_ref, up_ref, up_bias_ref, gain_ref, shift_ref):
    rank, width = up_ref.shape[1:]
    for k in range(2):
        down_ref[k] = sums_ref[k * rank : (k + 1) * rank, :width]
        up_ref[k] = sums_ref[(2 + k) * rank : (3 + k) * rank, :width]
    for n in range(width // 128):
        at = slice(128 * n, 128 * n + 128)
        tile = sums_ref[8 * n : 8 * n + 8, width:]
        up_bias_ref[:, at] = tile[0:2]
        gain_ref[:, at] = tile[2:4]
        shift_ref[:, at] = tile[4:6]
        if n == 0:
            down_bias_ref[...] = tile[6:8, :rank]
        if n == 1:
            ratio_ref[...] = tile[6:7, 0:2] / tile[6:7, 2:3]


def unpack(sums, rank):
    width = sums.shape[1] - 128
    shapes = [(1, 2), (2, rank, width), (2, rank), (2, rank, width)] + [(2, width)] * 3
    ratio, down, *rest = pl.pallas_call(
        unpack_kernel,
        out_shape=[jax.ShapeDtypeStruct(shape, jnp.float32) for shape in shapes],
        name="unpack",
    )(sums)
    return (ratio.reshape(2), jnp.transpose(down, (0, 2, 1)), *rest)


def row_mean(x):
    return jnp.mean(x, axis=-1, keepdims=True)


def col_sum(x):
    return jnp.sum(x, axis=0, keepdims=True)


def layer_norm(u, gain, shift):
    centred = u - row_mean(u)
    scale = lax.rsqrt(row_mean(centred * centred) + EPS_NORM)
    hat = centred * scale
    return hat, scale, hat * gain + shift


def layer_norm_grad(hat, scale, gain, grad):
    gg = grad * gain
    return scale * (gg - row_mean(gg) - hat * row_mean(gg * hat))


def middle_kernel(
    ff,
    chunk,
    ctx_ref,
    hid_ref,
    og_ref,
    seg_ref,
    wo_ref,
    we_ref,
    wr_ref,
    down_ref,
    down_bias_ref,
    up_ref,
    up_bias_ref,
    gain_ref,
    shift_ref,
    out_ref,
    sog_ref,
    cg_ref,
    sums_ref,
    small_ref,
    slope_ref,
    normed_ref,
    acc_ref,
):
    rank = up_ref.shape[1]
    width = up_ref.shape[2]

    @pl.when(pl.program_id(0) == 0)
    def _():
        sums_ref[...] = jnp.zeros_like(sums_ref)
        small_ref[...] = jnp.zeros_like(small_ref)

    def adapter(k, a):
        a_low = a.astype(jnp.bfloat16)
        act, slope = gelu_pair(dot_nt(a_low, down_ref[k]) + down_bias_ref[k : k + 1, :])
        act = act.astype(jnp.bfloat16)
        branch = dot(act, up_ref[k]) + up_bias_ref[k : k + 1, :]
        ratio = jnp.sqrt(row_mean(branch * branch)) / jnp.sqrt(row_mean(a * a) + EPS_RATIO)
        return branch, ratio, (a_low, act, slope)

    def add(row, value, start=0):
        small_ref[row : row + 1, start : start + value.shape[1]] += value

    def adapter_grad(k, kept, grad):
        a_low, act, slope = kept
        grad_low = grad.astype(jnp.bfloat16)
        hidden_grad = slope * dot_nt(grad_low, up_ref[k])
        hidden_grad = hidden_grad.astype(jnp.bfloat16)
        sums_ref[k * rank : (k + 1) * rank, :width] += dot_tn(hidden_grad, a_low)
        sums_ref[(2 + k) * rank : (3 + k) * rank, :width] += dot_tn(act, grad_low)
        add(k, col_sum(grad_low.astype(jnp.float32)))
        add(6 + k, col_sum(hidden_grad.astype(jnp.float32)))
        return (grad + dot(hidden_grad, down_ref[k])).astype(jnp.bfloat16)

    gain_one, gain_two = gain_ref[0:1, :], gain_ref[1:2, :]
    attended = dot(ctx_ref[...], wo_ref[...])
    branch, ratio_one, kept_one = adapter(0, attended)
    hat_one, scale_one, normed = layer_norm(
        hid_ref[...].astype(jnp.float32) + attended + branch, gain_one, shift_ref[0:1, :]
    )
    normed_ref[...] = normed.astype(jnp.bfloat16)
    acc_ref[...] = jnp.zeros_like(acc_ref)

    def feed(c, _):
        at = cols(c * chunk, chunk)
        act, slope = gelu_pair(dot(normed_ref[...], we_ref[:, at]))
        slope_ref[:, at] = slope
        acc_ref[...] += dot(act.astype(jnp.bfloat16), wr_ref[at, :])
        return 0

    lax.fori_loop(0, ff // chunk, feed, 0, unroll=2)
    feed_out = acc_ref[...]
    branch, ratio_two, kept_two = adapter(1, feed_out)
    hat_two, scale_two, final = layer_norm(normed + feed_out + branch, gain_two, shift_ref[1:2, :])
    out_ref[...] = final.astype(jnp.bfloat16)

    lane = lax.broadcasted_iota(jnp.int32, (1, 128), 1)
    ratios = jnp.where(lane == 0, ratio_one, jnp.where(lane == 1, ratio_two, 1.0))
    valid = (seg_ref[0] >= 0).astype(jnp.float32)
    stats = jnp.dot(
        jnp.broadcast_to(valid, (8, valid.shape[1])),
        ratios,
        precision=lax.Precision.HIGHEST,
        preferred_element_type=jnp.float32,
    )
    add(6, stats[0:1, :], 128)

    grad = og_ref[...].astype(jnp.float32)
    add(3, col_sum(grad * hat_two))
    add(5, col_sum(grad))
    sum_two_grad = layer_norm_grad(hat_two, scale_two, gain_two, grad)
    normed_ref[...] = adapter_grad(1, kept_two, sum_two_grad)
    acc_ref[...] = sum_two_grad

    def feed_grad(c, _):
        at = cols(c * chunk, chunk)
        inner_grad = slope_ref[:, at] * dot_nt(normed_ref[...], wr_ref[at, :])
        acc_ref[...] += dot_nt(inner_grad.astype(jnp.bfloat16), we_ref[:, at])
        return 0

    lax.fori_loop(0, ff // chunk, feed_grad, 0, unroll=2)
    grad = acc_ref[...]
    add(2, col_sum(grad * hat_one))
    add(4, col_sum(grad))
    sum_one_grad = layer_norm_grad(hat_one, scale_one, gain_one, grad)
    sog_ref[...] = sum_one_grad
    attended_grad = adapter_grad(0, kept_one, sum_one_grad)
    cg_ref[...] = dot_nt(attended_grad, wo_ref[...]).astype(jnp.bfloat16)

    @pl.when(pl.program_id(0) == pl.num_programs(0) - 1)
    def _():
        for n in range(width // 128):
            sums_ref[8 * n : 8 * n + 8, width:] = small_ref[:, 128 * n : 128 * n + 128]


TILE = 512
CHUNK = 512
SUM_ROWS = 256


def middle(ctx, hidden, output_grad, seg_ids, frozen, params):
    rows, width = hidden.shape
    weight_out, weight_expand, weight_reduce = frozen
    ff = weight_expand.shape[1]
    seg_tiles = seg_ids.reshape(rows // TILE, 1, TILE)
    whole = [weight_out, weight_expand, weight_reduce, *params]

    def tile_spec(n):
        return pl.BlockSpec((TILE, n), lambda i: (i, 0))

    def whole_spec(x):
        return pl.BlockSpec(x.shape, lambda i: (0,) * x.ndim, pipeline_mode=pl.Buffered(1))

    return pl.pallas_call(
        lambda *refs: middle_kernel(ff, CHUNK, *refs),
        grid=(rows // TILE,),
        out_shape=[
            jax.ShapeDtypeStruct((rows, width), jnp.bfloat16),
            jax.ShapeDtypeStruct((rows, width), jnp.float32),
            jax.ShapeDtypeStruct((rows, width), jnp.bfloat16),
            jax.ShapeDtypeStruct((SUM_ROWS, width + 128), jnp.float32),
        ],
        in_specs=[tile_spec(width)] * 3
        + [pl.BlockSpec((1, 1, TILE), lambda i: (i, 0, 0))]
        + [whole_spec(x) for x in whole],
        out_specs=[tile_spec(width)] * 3 + [pl.BlockSpec((SUM_ROWS, width + 128), lambda i: (0, 0))],
        scratch_shapes=[
            pltpu.VMEM((8, width), jnp.float32),
            pltpu.VMEM((TILE, ff), jnp.float32),
            pltpu.VMEM((TILE, width), jnp.bfloat16),
            pltpu.VMEM((TILE, width), jnp.float32),
        ],
        compiler_params=pltpu.CompilerParams(vmem_limit_bytes=VMEM_LIMIT),
        cost_estimate=pl.CostEstimate(
            flops=4 * rows * width * (width + 2 * ff),
            bytes_accessed=14 * rows * width + 2 * width * (width + 2 * ff),
            transcendentals=2 * rows * ff,
        ),
        name="middle",
    )(ctx, hidden, output_grad, seg_tiles, *whole)


def body(
    hidden_states,
    segment_ids,
    input_weight,
    output_weight,
    expand_weight,
    reduce_weight,
    adapter_down,
    adapter_down_bias,
    adapter_up,
    adapter_up_bias,
    norm_gain,
    norm_shift,
    output_grad,
):
    if gather_fits([input_weight]):
        weight_in = gather_first(input_weight)
    else:
        weight_in = lax.all_gather(input_weight, "dp", axis=0, tiled=True)
    seg_rows = segment_ids.reshape(-1, 1, SEQ_LEN)
    shards = [output_weight, expand_weight, reduce_weight]
    qkv, ctx, frozen = attend_forward(hidden_states, seg_rows, weight_in, shards)
    params = (
        jnp.transpose(adapter_down, (0, 2, 1)),
        adapter_down_bias,
        adapter_up,
        adapter_up_bias,
        norm_gain,
        norm_shift,
    )
    output, sum_one_grad, ctx_grad, sums = middle(
        ctx, hidden_states, output_grad, segment_ids, frozen, params
    )
    input_grad, sums = attend_backward(qkv, ctx_grad, seg_rows, sum_one_grad, weight_in, sums)
    return (output, input_grad, *unpack(sums, adapter_up.shape[1]))


def solution(mesh):
    tokens = P(("dp", "head"), None)
    in_specs = (tokens, P(("dp", "head"))) + (P("dp", None),) * 4 + (P(),) * 6 + (tokens,)
    out_specs = (tokens, tokens) + (P(),) * 7
    return jax.shard_map(body, mesh=mesh, in_specs=in_specs, out_specs=out_specs, check_vma=False)
```

```python
import jax
import jax.numpy as jnp
from jax import lax
from jax.experimental import pallas as pl
from jax.experimental.pallas import tpu as pltpu
from jax.sharding import PartitionSpec as P

MESH = pl.DeviceIdType.MESH
PLANE = 4


def gather_stages(depth, z_first, shards, outs, own_sem, send_sem, recv_sem, pair_send, pair_recv):
    me = lax.axis_index("dp")
    core = lax.axis_index("head")
    z = me // PLANE
    step_a = 1 + core
    step_b = 2 - core
    a = (me // step_a) % 2
    b = (me // step_b) % 2
    peer_a = z * PLANE + (1 - a) * step_a + b * step_b
    peer_b = z * PLANE + a * step_a + (1 - b) * step_b
    up, down = me + PLANE, me - PLANE
    partner = 1 - core

    def has_up():
        return z < depth - 1

    def has_down():
        return z > 0

    count = len(outs)
    pending = []

    def owner(z_of, a_of, b_of):
        return z_of * PLANE + a_of * step_a + b_of * step_b

    def guarded(cond, act):
        if cond is None:
            act()
        else:
            pl.when(cond())(act)

    def send(cond, w, piece, src, dst, direction, slot, target):
        def copy():
            return pltpu.make_async_remote_copy(
                src_ref=src,
                dst_ref=dst,
                send_sem=send_sem.at[w, direction, slot],
                recv_sem=recv_sem.at[w, piece],
                device_id={"dp": target},
                device_id_type=MESH,
            )

        guarded(cond, lambda: copy().start())
        pending.append((cond, w, send_sem, (w, direction, slot)))

    def hand(cond, w, piece, view):
        def copy():
            return pltpu.make_async_remote_copy(
                src_ref=view,
                dst_ref=view,
                send_sem=pair_send.at[w, piece],
                recv_sem=pair_recv.at[w, piece],
                device_id={"head": partner},
                device_id_type=MESH,
            )

        guarded(cond, lambda: copy().start())

    def view_of(w, piece, side):
        half = outs[w].shape[2] // 2
        return outs[w].at[piece, :, pl.ds(pl.multiple_of(side * half, 128), half)]

    def wait(sem, view):
        pltpu.make_async_copy(view, view, sem).wait()

    def arrive(cond, w, piece):
        view = view_of(w, piece, core)
        guarded(cond, lambda: wait(recv_sem.at[w, piece], view))
        return view

    def start():
        barrier = pltpu.get_barrier_semaphore()

        def greet(cond, target):
            guarded(
                cond,
                lambda: pl.semaphore_signal(
                    barrier, inc=1, device_id=target, device_id_type=MESH
                ),
            )

        greet(None, {"dp": peer_a})
        greet(None, {"dp": peer_b})
        greet(None, {"head": partner})
        greet(has_up, {"dp": up})
        greet(has_down, {"dp": down})
        pl.semaphore_wait(barrier, 3 + has_up().astype(jnp.int32) + has_down().astype(jnp.int32))
        for w in range(count):
            half = outs[w].shape[2] // 2
            src = shards[w].at[:, pl.ds(pl.multiple_of(core * half, 128), half)]
            view = view_of(w, me, core)
            send(None, w, me, src, view, 0, 0, peer_a)
            send(has_up, w, me, src, view, 1, 0, up)
            send(has_down, w, me, src, view, 2, 0, down)
            send(None, w, me, src, view, 3, 0, peer_b)
        for w in range(count):
            pltpu.make_async_copy(shards[w], outs[w].at[me], own_sem.at[w]).start()

    def first(w):
        if z_first[w]:
            return
        view = arrive(None, w, peer_a)
        send(has_up, w, peer_a, view, view, 1, 1, up)
        send(has_down, w, peer_a, view, view, 2, 1, down)
        send(None, w, peer_a, view, view, 3, 1, peer_b)
        hand(None, w, peer_a, view)

    def line(w, dist):
        for k, a_of in enumerate((a,) if z_first[w] else (a, 1 - a)):
            slot = 2 * dist + k
            for above in (False, True):
                z_of = z + dist if above else z - dist

                def there(above=above):
                    return z + dist < depth if above else z >= dist

                def onward(above=above):
                    inner = z > 0 if above else z < depth - 1
                    return jnp.logical_and(there(above), inner)

                piece = owner(z_of, a_of, b)
                view = arrive(there, w, piece)
                if above:
                    send(onward, w, piece, view, view, 2, slot, down)
                else:
                    send(onward, w, piece, view, view, 1, slot, up)
                late = 2 * depth * above + slot
                if z_first[w]:
                    send(there, w, piece, view, view, 0, late, peer_a)
                send(there, w, piece, view, view, 3, late, peer_b)
                hand(there, w, piece, view)

    def across(w):
        for z_of in range(depth):
            piece = owner(z_of, 1 - a, b)
            view = arrive(None, w, piece)
            send(None, w, piece, view, view, 3, 4 * depth + z_of, peer_b)
            hand(None, w, piece, view)

    def last(w):
        for z_of in range(depth):
            for a_of in range(2):
                piece = owner(z_of, a_of, 1 - b)
                hand(None, w, piece, arrive(None, w, piece))

    def finish():
        for w in range(count):
            wait(own_sem.at[w], outs[w].at[me])
            for z_of in range(depth):
                for a_of in range(2):
                    for b_of in range(2):
                        piece = owner(z_of, a_of, b_of)

                        def pair(w=w, piece=piece):
                            wait(pair_recv.at[w, piece], view_of(w, piece, partner))
                            wait(pair_send.at[w, piece], view_of(w, piece, core))

                        pl.when(piece != me)(pair)
        for cond, w, sem, at in pending:
            guarded(cond, lambda: wait(sem.at[at], view_of(w, me, core)))

    def firsts():
        for w in range(count):
            first(w)

    stages = [start, firsts]
    for dist in range(1, depth):
        for w in range(count):
            stages.append(lambda w=w, dist=dist: line(w, dist))
    for w in range(count):
        if z_first[w]:
            stages.append(lambda w=w: across(w))
    for w in range(count):
        stages.append(lambda w=w: last(w))
    return stages + [finish]


def gather_scratch(count, size):
    return [
        pltpu.SemaphoreType.DMA((count,)),
        pltpu.SemaphoreType.DMA((count, 4, 5 * (size // PLANE))),
        pltpu.SemaphoreType.DMA((count, size)),
        pltpu.SemaphoreType.DMA((count, size)),
        pltpu.SemaphoreType.DMA((count, size)),
    ]


def gather_fits(weights):
    size = lax.axis_size("dp")
    return (
        size % PLANE == 0
        and size > PLANE
        and all(w.shape[0] % 16 == 0 and w.shape[1] % 256 == 0 for w in weights)
    )


def gather_shapes(weights):
    size = lax.axis_size("dp")
    return [jax.ShapeDtypeStruct((size,) + w.shape, w.dtype) for w in weights]


def join(pieces):
    return pieces.reshape(-1, pieces.shape[-1])


def gather_kernel(depth, *refs):
    for stage in gather_stages(depth, (False,), refs[:1], refs[1:2], *refs[2:]):
        stage()


def gather_first(weight):
    size = lax.axis_size("dp")
    gathered = pl.pallas_call(
        lambda *refs: gather_kernel(size // PLANE, *refs),
        out_shape=gather_shapes([weight]),
        in_specs=[pl.BlockSpec(memory_space=pltpu.VMEM)],
        out_specs=[pl.BlockSpec(memory_space=pl.ANY)],
        scratch_shapes=gather_scratch(1, size),
        compiler_params=pltpu.CompilerParams(collective_id=0, has_side_effects=True),
        name="gather_first",
    )(weight)
    return join(gathered[0])


HEAD_DIM = 64
SEQ_LEN = 512
PAIR = 2 * HEAD_DIM
LOG2E = 1.4426950408889634
EPS_NORM = 1e-12
EPS_RATIO = 1e-06
SCORE_SCALE = 0.125
VMEM_LIMIT = 60 * 1024 * 1024

TAIL_POLY = (
    0.09973556672,
    0.09973643158,
    0.09346635627,
    0.08160309818,
    0.05897520771,
    0.06369893559,
    -0.03171721207,
    0.0955967654,
    -0.08087713545,
    0.01978196913,
)
INV_SQRT_2PI = 0.3989422804014327


def gelu_pair(x):
    t = 1.0 / (1.0 + 0.25 * jnp.abs(x))
    poly = jnp.full_like(t, TAIL_POLY[-1])
    for coef in TAIL_POLY[-2::-1]:
        poly = poly * t + coef
    bell = jnp.exp2(x * x * (-0.5 * LOG2E))
    below = bell * (t * poly)
    cdf = jnp.where(x >= 0, 1.0 - below, below)
    return x * cdf, cdf + x * (bell * INV_SQRT_2PI)


def dot(a, b):
    return jnp.dot(a, b, preferred_element_type=jnp.float32)


def dot_nt(a, b):
    return lax.dot_general(a, b, (((1,), (1,)), ((), ())), preferred_element_type=jnp.float32)


def dot_tn(a, b):
    return lax.dot_general(a, b, (((0,), (0,)), ((), ())), preferred_element_type=jnp.float32)


def score_bias(seg_row):
    across = jnp.broadcast_to(seg_row, (SEQ_LEN, SEQ_LEN))
    tall = jnp.broadcast_to(seg_row, (PAIR, SEQ_LEN)).T
    along = jnp.concatenate([tall] * (SEQ_LEN // PAIR), axis=1)
    row = lax.broadcasted_iota(jnp.int32, (SEQ_LEN, SEQ_LEN), 0)
    col = lax.broadcasted_iota(jnp.int32, (SEQ_LEN, SEQ_LEN), 1)
    allowed = ((across == along) & (across >= 0)) | (row == col)
    return jnp.where(allowed, 0.0, -1e30)


def head_lanes():
    lane = lax.broadcasted_iota(jnp.int32, (1, PAIR), 1)
    first = (lane < HEAD_DIM).astype(jnp.float32)
    return lane < HEAD_DIM, (first.astype(jnp.bfloat16), (1.0 - first).astype(jnp.bfloat16))


def cols(start, width):
    return pl.ds(pl.multiple_of(start, 128), width)


def attend_kernel(width, depth, *refs):
    hid_ref, seg_ref, w_ref = refs[:3]
    if depth:
        shards, (qkv_ref, ctx_ref), outs, bias_ref = refs[3:6], refs[6:8], refs[8:11], refs[11]
        start, *stages, finish = gather_stages(depth, Z_FIRST, shards, outs, *refs[12:])
        pl.when(pl.program_id(0) == 0)(start)
    else:
        qkv_ref, ctx_ref, bias_ref = refs[3:]
        stages = []
    turn = pl.program_id(0)
    pairs = width // PAIR
    step = 256

    def project(c, _):
        at = cols(c * step, step)
        qkv_ref[:, at] = dot(hid_ref[...], w_ref[:, at]).astype(jnp.bfloat16)
        return 0

    lax.fori_loop(0, 3 * width // step, project, 0)
    bias_ref[...] = score_bias(seg_ref[0])
    low, masks = head_lanes()

    def pair(h, _):
        for n, stage in enumerate(stages[: SLOTS]):
            pl.when(turn * pairs + h == n)(stage)
        q = qkv_ref[:, cols(h * PAIR, PAIR)]
        k = qkv_ref[:, cols(width + h * PAIR, PAIR)]
        v = qkv_ref[:, cols(2 * width + h * PAIR, PAIR)]
        v_ones = jnp.concatenate([v, jnp.ones_like(v)], axis=1)
        parts = []
        for mask in masks:
            s = dot_nt(q * mask, k) * (SCORE_SCALE * LOG2E) + bias_ref[...]
            e = jnp.exp2(s - jnp.max(s, axis=1, keepdims=True)).astype(jnp.bfloat16)
            o = dot(e, v_ones)
            parts.append(o[:, :PAIR] / o[:, PAIR:])
        ctx_ref[:, cols(h * PAIR, PAIR)] = jnp.where(low, parts[0], parts[1]).astype(jnp.bfloat16)
        return 0

    lax.fori_loop(0, pairs, pair, 0)
    if stages:

        @pl.when(turn == pl.num_programs(0) - 1)
        def _():
            for stage in stages[SLOTS:]:
                stage()
            finish()


Z_FIRST = (False, False, True)
SLOTS = 12


def attend_forward(hidden, seg_rows, weight_in, shards):
    rows, width = hidden.shape
    size = lax.axis_size("dp")
    fits = gather_fits(shards) and rows // SEQ_LEN * (width // PAIR) >= SLOTS
    depth = size // PLANE if fits else 0
    operands = [hidden, seg_rows, weight_in]
    in_specs = [
        pl.BlockSpec((SEQ_LEN, width), lambda i: (i, 0)),
        pl.BlockSpec((1, 1, SEQ_LEN), lambda i: (i, 0, 0)),
        pl.BlockSpec((width, 3 * width), lambda i: (0, 0)),
    ]
    out_shape = [
        jax.ShapeDtypeStruct((rows, 3 * width), jnp.bfloat16),
        jax.ShapeDtypeStruct((rows, width), jnp.bfloat16),
    ]
    out_specs = [
        pl.BlockSpec((SEQ_LEN, 3 * width), lambda i: (i, 0)),
        pl.BlockSpec((SEQ_LEN, width), lambda i: (i, 0)),
    ]
    scratch = [pltpu.VMEM((SEQ_LEN, SEQ_LEN), jnp.float32)]
    settings = {"vmem_limit_bytes": VMEM_LIMIT}
    if fits:
        operands += shards
        in_specs += [pl.BlockSpec(w.shape, lambda i: (0, 0)) for w in shards]
        out_shape += gather_shapes(shards)
        out_specs += [pl.BlockSpec(memory_space=pl.ANY)] * len(shards)
        scratch += gather_scratch(len(shards), size)
        settings |= {"collective_id": 2, "has_side_effects": True}
    qkv, ctx, *gathered = pl.pallas_call(
        lambda *refs: attend_kernel(width, depth, *refs),
        grid=(rows // SEQ_LEN,),
        out_shape=out_shape,
        in_specs=in_specs,
        out_specs=out_specs,
        scratch_shapes=scratch,
        compiler_params=pltpu.CompilerParams(**settings),
        cost_estimate=pl.CostEstimate(
            flops=rows * width * (6 * width + 4 * SEQ_LEN),
            bytes_accessed=2 * rows * 5 * width + 6 * width * width,
            transcendentals=rows * SEQ_LEN * width // HEAD_DIM,
        ),
        name="attend_forward",
    )(*operands)
    if not fits:
        return qkv, ctx, [lax.all_gather(w, "dp", axis=0, tiled=True) for w in shards]
    return qkv, ctx, [join(pieces) for pieces in gathered]


def reduce_phases(depth, sums_ref, out_ref, first, second, third, fourth, acc, total, send_sem, recv_sem):
    me = lax.axis_index("dp")
    core = lax.axis_index("head")
    z = me // PLANE
    step_a, step_b = 1 + core, 2 - core
    a, b = (me // step_a) % 2, (me // step_b) % 2
    peer_a = {"dp": z * PLANE + (1 - a) * step_a + b * step_b}
    peer_b = {"dp": z * PLANE + a * step_a + (1 - b) * step_b}
    partner = {"head": 1 - core}
    ring = [{"dp": (z + d) % depth * PLANE + me % PLANE} for d in range(1, depth)]
    half = sums_ref.shape[0] // 2
    quarter, eighth = half // 2, half // 4
    piece = eighth // depth

    def rows(start, size):
        return pl.ds(pl.multiple_of(start, 8), size)

    def send(slot, src, dst, target):
        copy = pltpu.make_async_remote_copy(
            src_ref=src,
            dst_ref=dst,
            send_sem=send_sem.at[slot],
            recv_sem=recv_sem.at[slot],
            device_id=target,
            device_id_type=MESH,
        )
        copy.start()

    def wait(sem, view):
        pltpu.make_async_copy(view, view, sem).wait()

    def arrive(slot, view):
        wait(recv_sem.at[slot], view)
        return view

    base_a = core * half + a * quarter
    base_b = base_a + b * eighth
    local_b = a * quarter + b * eighth
    one, two, three, back_b, back_a, back = range(6)
    out_z = [6 + d for d in range(depth - 1)]
    back_z = [5 + depth + d for d in range(depth - 1)]

    def start():
        barrier = pltpu.get_barrier_semaphore()
        for target in [partner, peer_a, peer_b] + ring:
            pl.semaphore_signal(barrier, inc=1, device_id=target, device_id_type=MESH)
        pl.semaphore_wait(barrier, 2 + depth)
        send(one, sums_ref.at[rows((1 - core) * half, half), :], first, partner)

    def reduce_a():
        arrive(one, first)
        acc[...] = sums_ref[rows(core * half, half), :] + first[...]
        send(two, acc.at[rows((1 - a) * quarter, quarter), :], second, peer_a)

    def reduce_b():
        arrive(two, second)
        acc[rows(a * quarter, quarter), :] += second[...]
        send(three, acc.at[rows(a * quarter + (1 - b) * eighth, eighth), :], third, peer_b)

    def reduce_z():
        arrive(three, third)
        acc[rows(local_b, eighth), :] += third[...]
        for d in range(depth - 1):
            owner = (z + 1 + d) % depth
            src = acc.at[rows(local_b + owner * piece, piece), :]
            send(out_z[d], src, fourth.at[d], ring[d])

    def finish():
        mine = acc[rows(local_b + z * piece, piece), :]
        for d in range(depth - 1):
            arrive(out_z[d], fourth.at[d])
            mine += fourth[d]
        view = total.at[rows(base_b + z * piece, piece), :]
        view[...] = mine
        for d in range(depth - 1):
            send(back_z[d], view, view, ring[d])

    def return_b():
        for d in range(depth - 1):
            sender = (z + depth - 1 - d) % depth
            arrive(back_z[d], total.at[rows(base_b + sender * piece, piece), :])
        view = total.at[rows(base_b, eighth), :]
        send(back_b, view, view, peer_b)

    def return_a():
        arrive(back_b, total.at[rows(base_a + (1 - b) * eighth, eighth), :])
        view = total.at[rows(base_a, quarter), :]
        send(back_a, view, view, peer_a)

    def return_core():
        arrive(back_a, total.at[rows(core * half + (1 - a) * quarter, quarter), :])
        view = total.at[rows(core * half, half), :]
        send(back, view, view, partner)

    def end():
        arrive(back, total.at[rows((1 - core) * half, half), :])
        out_ref[...] = total[...]
        for slot, view in [
            (one, first),
            (two, second),
            (three, third),
            (back_b, third),
            (back_a, second),
            (back, first),
        ]:
            wait(send_sem.at[slot], view)
        for slot in out_z + back_z:
            wait(send_sem.at[slot], fourth.at[0])

    return [start, reduce_a, reduce_b, reduce_z, finish, return_b, return_a, return_core, end]


def attend_grad_kernel(width, depth, *refs):
    qkv_ref, cg_ref, seg_ref, sog_ref, w_ref = refs[:5]
    if depth:
        sums_ref, out_ref, reduced_ref, grad_ref, bias_ref = refs[5:10]
        *phases, end = reduce_phases(depth, sums_ref, reduced_ref, *refs[10:])
    else:
        out_ref, grad_ref, bias_ref = refs[5:]
        phases = []
    turn = pl.program_id(0)
    pairs = width // PAIR
    bias_ref[...] = score_bias(seg_ref[0])
    low, masks = head_lanes()

    def pair(h, _):
        for n, phase in zip(REDUCE_SLOTS, phases):
            pl.when(turn * pairs + h == n)(phase)
        q = qkv_ref[:, cols(h * PAIR, PAIR)]
        k = qkv_ref[:, cols(width + h * PAIR, PAIR)]
        v = qkv_ref[:, cols(2 * width + h * PAIR, PAIR)]
        g = cg_ref[:, cols(h * PAIR, PAIR)]
        parts = []
        for mask in masks:
            s = dot_nt(k * mask, q) * (SCORE_SCALE * LOG2E) + bias_ref[...]
            e = jnp.exp2(s - jnp.max(s, axis=0, keepdims=True))
            p = e * (1.0 / jnp.sum(e, axis=0, keepdims=True))
            pg = dot_nt(v * mask, g)
            ds = (p * (pg - jnp.sum(p * pg, axis=0, keepdims=True))).astype(jnp.bfloat16)
            parts.append((dot_tn(ds, k), dot(ds, q), dot(p.astype(jnp.bfloat16), g)))
        for n, scale in enumerate((SCORE_SCALE, SCORE_SCALE, 1.0)):
            both = jnp.where(low, parts[0][n], parts[1][n]) * scale
            grad_ref[:, cols(n * width + h * PAIR, PAIR)] = both.astype(jnp.bfloat16)
        return 0

    lax.fori_loop(0, pairs, pair, 0)
    step = 256

    def back(c, _):
        at = cols(c * step, step)
        out_ref[:, at] = sog_ref[:, at] + dot_nt(grad_ref[...], w_ref[at, :])
        return 0

    lax.fori_loop(0, width // step, back, 0)
    if phases:
        pl.when(turn == pl.num_programs(0) - 1)(end)


REDUCE_SLOTS = (0, 1, 3, 4, 6, 8, 9, 11)


def attend_backward(qkv, ctx_grad, seg_rows, sum_one_grad, weight_in, sums):
    rows, width = ctx_grad.shape
    count, span = sums.shape
    size = lax.axis_size("dp")
    depth = size // PLANE
    fits = size % PLANE == 0 and count % (64 * depth) == 0 and rows // SEQ_LEN * (width // PAIR) > REDUCE_SLOTS[-1]
    fits = fits and depth > 1
    if not fits:
        depth = 0
    operands = [qkv, ctx_grad, seg_rows, sum_one_grad, weight_in]
    in_specs = [
        pl.BlockSpec((SEQ_LEN, 3 * width), lambda i: (i, 0)),
        pl.BlockSpec((SEQ_LEN, width), lambda i: (i, 0)),
        pl.BlockSpec((1, 1, SEQ_LEN), lambda i: (i, 0, 0)),
        pl.BlockSpec((SEQ_LEN, width), lambda i: (i, 0)),
        pl.BlockSpec((width, 3 * width), lambda i: (0, 0)),
    ]
    out_shape = [jax.ShapeDtypeStruct((rows, width), jnp.float32)]
    out_specs = [pl.BlockSpec((SEQ_LEN, width), lambda i: (i, 0))]
    scratch = [
        pltpu.VMEM((SEQ_LEN, 3 * width), jnp.bfloat16),
        pltpu.VMEM((SEQ_LEN, SEQ_LEN), jnp.float32),
    ]
    settings = {"vmem_limit_bytes": VMEM_LIMIT}
    if fits:
        operands.append(sums)
        in_specs.append(pl.BlockSpec((count, span), lambda i: (0, 0)))
        out_shape.append(jax.ShapeDtypeStruct((count, span), jnp.float32))
        out_specs.append(pl.BlockSpec((count, span), lambda i: (0, 0)))
        scratch += [
            pltpu.VMEM((count // 2, span), jnp.float32),
            pltpu.VMEM((count // 4, span), jnp.float32),
            pltpu.VMEM((count // 8, span), jnp.float32),
            pltpu.VMEM((depth - 1, count // 8 // depth, span), jnp.float32),
            pltpu.VMEM((count // 2, span), jnp.float32),
            pltpu.VMEM((count, span), jnp.float32),
            pltpu.SemaphoreType.DMA((4 + 2 * depth,)),
            pltpu.SemaphoreType.DMA((4 + 2 * depth,)),
        ]
        settings |= {"collective_id": 1, "has_side_effects": True}
    input_grad, *reduced = pl.pallas_call(
        lambda *refs: attend_grad_kernel(width, depth, *refs),
        grid=(rows // SEQ_LEN,),
        out_shape=out_shape,
        in_specs=in_specs,
        out_specs=out_specs,
        scratch_shapes=scratch,
        compiler_params=pltpu.CompilerParams(**settings),
        cost_estimate=pl.CostEstimate(
            flops=rows * width * (6 * width + 10 * SEQ_LEN),
            bytes_accessed=2 * rows * 8 * width + 6 * width * width,
            transcendentals=rows * SEQ_LEN * width // HEAD_DIM,
        ),
        name="attend_backward",
    )(*operands)
    return input_grad, reduced[0] if fits else lax.psum(sums, ("dp", "head"))


def unpack_kernel(sums_ref, ratio_ref, down_ref, down_bias_ref, up_ref, up_bias_ref, gain_ref, shift_ref):
    rank, width = up_ref.shape[1:]
    for k in range(2):
        down_ref[k] = sums_ref[k * rank : (k + 1) * rank, :width]
        up_ref[k] = sums_ref[(2 + k) * rank : (3 + k) * rank, :width]
    for n in range(width // 128):
        at = slice(128 * n, 128 * n + 128)
        tile = sums_ref[8 * n : 8 * n + 8, width:]
        up_bias_ref[:, at] = tile[0:2]
        gain_ref[:, at] = tile[2:4]
        shift_ref[:, at] = tile[4:6]
        if n == 0:
            down_bias_ref[...] = tile[6:8, :rank]
        if n == 1:
            ratio_ref[...] = tile[6:7, 0:2] / tile[6:7, 2:3]


def unpack(sums, rank):
    width = sums.shape[1] - 128
    shapes = [(1, 2), (2, rank, width), (2, rank), (2, rank, width)] + [(2, width)] * 3
    ratio, down, *rest = pl.pallas_call(
        unpack_kernel,
        out_shape=[jax.ShapeDtypeStruct(shape, jnp.float32) for shape in shapes],
        name="unpack",
    )(sums)
    return (ratio.reshape(2), jnp.transpose(down, (0, 2, 1)), *rest)


def row_mean(x):
    return jnp.mean(x, axis=-1, keepdims=True)


def col_sum(x):
    return jnp.sum(x, axis=0, keepdims=True)


def layer_norm(u, gain, shift):
    centred = u - row_mean(u)
    scale = lax.rsqrt(row_mean(centred * centred) + EPS_NORM)
    hat = centred * scale
    return hat, scale, hat * gain + shift


def layer_norm_grad(hat, scale, gain, grad):
    gg = grad * gain
    return scale * (gg - row_mean(gg) - hat * row_mean(gg * hat))


def middle_kernel(
    ff,
    chunk,
    ctx_ref,
    hid_ref,
    og_ref,
    seg_ref,
    wo_ref,
    we_ref,
    wr_ref,
    down_ref,
    down_bias_ref,
    up_ref,
    up_bias_ref,
    gain_ref,
    shift_ref,
    out_ref,
    sog_ref,
    cg_ref,
    sums_ref,
    small_ref,
    slope_ref,
    normed_ref,
    acc_ref,
):
    rank = up_ref.shape[1]
    width = up_ref.shape[2]

    @pl.when(pl.program_id(0) == 0)
    def _():
        sums_ref[...] = jnp.zeros_like(sums_ref)
        small_ref[...] = jnp.zeros_like(small_ref)

    def adapter(k, a):
        a_low = a.astype(jnp.bfloat16)
        act, slope = gelu_pair(dot_nt(a_low, down_ref[k]) + down_bias_ref[k : k + 1, :])
        act = act.astype(jnp.bfloat16)
        branch = dot(act, up_ref[k]) + up_bias_ref[k : k + 1, :]
        ratio = jnp.sqrt(row_mean(branch * branch)) / jnp.sqrt(row_mean(a * a) + EPS_RATIO)
        return branch, ratio, (a_low, act, slope)

    def add(row, value, start=0):
        small_ref[row : row + 1, start : start + value.shape[1]] += value

    def adapter_grad(k, kept, grad):
        a_low, act, slope = kept
        grad_low = grad.astype(jnp.bfloat16)
        hidden_grad = slope * dot_nt(grad_low, up_ref[k])
        hidden_grad = hidden_grad.astype(jnp.bfloat16)
        sums_ref[k * rank : (k + 1) * rank, :width] += dot_tn(hidden_grad, a_low)
        sums_ref[(2 + k) * rank : (3 + k) * rank, :width] += dot_tn(act, grad_low)
        add(k, col_sum(grad_low.astype(jnp.float32)))
        add(6 + k, col_sum(hidden_grad.astype(jnp.float32)))
        return (grad + dot(hidden_grad, down_ref[k])).astype(jnp.bfloat16)

    gain_one, gain_two = gain_ref[0:1, :], gain_ref[1:2, :]
    attended = dot(ctx_ref[...], wo_ref[...])
    branch, ratio_one, kept_one = adapter(0, attended)
    hat_one, scale_one, normed = layer_norm(
        hid_ref[...].astype(jnp.float32) + attended + branch, gain_one, shift_ref[0:1, :]
    )
    normed_ref[...] = normed.astype(jnp.bfloat16)
    acc_ref[...] = jnp.zeros_like(acc_ref)

    def feed(c, _):
        at = cols(c * chunk, chunk)
        act, slope = gelu_pair(dot(normed_ref[...], we_ref[:, at]))
        slope_ref[:, at] = slope
        acc_ref[...] += dot(act.astype(jnp.bfloat16), wr_ref[at, :])
        return 0

    lax.fori_loop(0, ff // chunk, feed, 0, unroll=2)
    feed_out = acc_ref[...]
    branch, ratio_two, kept_two = adapter(1, feed_out)
    hat_two, scale_two, final = layer_norm(normed + feed_out + branch, gain_two, shift_ref[1:2, :])
    out_ref[...] = final.astype(jnp.bfloat16)

    lane = lax.broadcasted_iota(jnp.int32, (1, 128), 1)
    ratios = jnp.where(lane == 0, ratio_one, jnp.where(lane == 1, ratio_two, 1.0))
    valid = (seg_ref[0] >= 0).astype(jnp.float32)
    stats = jnp.dot(
        jnp.broadcast_to(valid, (8, valid.shape[1])),
        ratios,
        precision=lax.Precision.HIGHEST,
        preferred_element_type=jnp.float32,
    )
    add(6, stats[0:1, :], 128)

    grad = og_ref[...].astype(jnp.float32)
    add(3, col_sum(grad * hat_two))
    add(5, col_sum(grad))
    sum_two_grad = layer_norm_grad(hat_two, scale_two, gain_two, grad)
    normed_ref[...] = adapter_grad(1, kept_two, sum_two_grad)
    acc_ref[...] = sum_two_grad

    def feed_grad(c, _):
        at = cols(c * chunk, chunk)
        inner_grad = slope_ref[:, at] * dot_nt(normed_ref[...], wr_ref[at, :])
        acc_ref[...] += dot_nt(inner_grad.astype(jnp.bfloat16), we_ref[:, at])
        return 0

    lax.fori_loop(0, ff // chunk, feed_grad, 0, unroll=2)
    grad = acc_ref[...]
    add(2, col_sum(grad * hat_one))
    add(4, col_sum(grad))
    sum_one_grad = layer_norm_grad(hat_one, scale_one, gain_one, grad)
    sog_ref[...] = sum_one_grad
    attended_grad = adapter_grad(0, kept_one, sum_one_grad)
    cg_ref[...] = dot_nt(attended_grad, wo_ref[...]).astype(jnp.bfloat16)

    @pl.when(pl.program_id(0) == pl.num_programs(0) - 1)
    def _():
        for n in range(width // 128):
            sums_ref[8 * n : 8 * n + 8, width:] = small_ref[:, 128 * n : 128 * n + 128]


TILE = 512
CHUNK = 512
SUM_ROWS = 256


def middle(ctx, hidden, output_grad, seg_ids, frozen, params):
    rows, width = hidden.shape
    weight_out, weight_expand, weight_reduce = frozen
    ff = weight_expand.shape[1]
    seg_tiles = seg_ids.reshape(rows // TILE, 1, TILE)
    whole = [weight_out, weight_expand, weight_reduce, *params]

    def tile_spec(n):
        return pl.BlockSpec((TILE, n), lambda i: (i, 0))

    def whole_spec(x):
        return pl.BlockSpec(x.shape, lambda i: (0,) * x.ndim, pipeline_mode=pl.Buffered(1))

    return pl.pallas_call(
        lambda *refs: middle_kernel(ff, CHUNK, *refs),
        grid=(rows // TILE,),
        out_shape=[
            jax.ShapeDtypeStruct((rows, width), jnp.bfloat16),
            jax.ShapeDtypeStruct((rows, width), jnp.float32),
            jax.ShapeDtypeStruct((rows, width), jnp.bfloat16),
            jax.ShapeDtypeStruct((SUM_ROWS, width + 128), jnp.float32),
        ],
        in_specs=[tile_spec(width)] * 3
        + [pl.BlockSpec((1, 1, TILE), lambda i: (i, 0, 0))]
        + [whole_spec(x) for x in whole],
        out_specs=[tile_spec(width)] * 3 + [pl.BlockSpec((SUM_ROWS, width + 128), lambda i: (0, 0))],
        scratch_shapes=[
            pltpu.VMEM((8, width), jnp.float32),
            pltpu.VMEM((TILE, ff), jnp.float32),
            pltpu.VMEM((TILE, width), jnp.bfloat16),
            pltpu.VMEM((TILE, width), jnp.float32),
        ],
        compiler_params=pltpu.CompilerParams(vmem_limit_bytes=VMEM_LIMIT),
        cost_estimate=pl.CostEstimate(
            flops=4 * rows * width * (width + 2 * ff),
            bytes_accessed=14 * rows * width + 2 * width * (width + 2 * ff),
            transcendentals=2 * rows * ff,
        ),
        name="middle",
    )(ctx, hidden, output_grad, seg_tiles, *whole)


def body(
    hidden_states,
    segment_ids,
    input_weight,
    output_weight,
    expand_weight,
    reduce_weight,
    adapter_down,
    adapter_down_bias,
    adapter_up,
    adapter_up_bias,
    norm_gain,
    norm_shift,
    output_grad,
):
    if gather_fits([input_weight]):
        weight_in = gather_first(input_weight)
    else:
        weight_in = lax.all_gather(input_weight, "dp", axis=0, tiled=True)
    seg_rows = segment_ids.reshape(-1, 1, SEQ_LEN)
    shards = [output_weight, expand_weight, reduce_weight]
    qkv, ctx, frozen = attend_forward(hidden_states, seg_rows, weight_in, shards)
    params = (
        jnp.transpose(adapter_down, (0, 2, 1)),
        adapter_down_bias,
        adapter_up,
        adapter_up_bias,
        norm_gain,
        norm_shift,
    )
    output, sum_one_grad, ctx_grad, sums = middle(
        ctx, hidden_states, output_grad, segment_ids, frozen, params
    )
    input_grad, sums = attend_backward(qkv, ctx_grad, seg_rows, sum_one_grad, weight_in, sums)
    return (output, input_grad, *unpack(sums, adapter_up.shape[1]))


def solution(mesh):
    tokens = P(("dp", "head"), None)
    in_specs = (tokens, P(("dp", "head"))) + (P("dp", None),) * 4 + (P(),) * 6 + (tokens,)
    out_specs = (tokens, tokens) + (P(),) * 7
    return jax.shard_map(body, mesh=mesh, in_specs=in_specs, out_specs=out_specs, check_vma=False)
```
